512 devices in a mesh: tm: 16 (over z, core), lat: 8 (over x, y_hi), lon: 4 (over y_lo).
Axes of the slice: x: 4, y: 8 (y_hi: 2, y_lo: 4; y = y_hi * 4 + y_lo), z: 8, core: 2. Of those that a mesh axis runs over, the one named last changes fastest.
Arguments:
- tokens: bfloat16 [64, 32, 32, 768], P('tm', 'lat', 'lon'), may hold values from -40 to 40
- key_count: int32 [16, 8, 8], P('tm', 'lat', 'lon'), may hold values from 1 to 64
- norm_gain: float32 [768], replicated, may hold values from 0.1 to 1.9
- qkv_weight: bfloat16 [3, 768, 384], replicated, may hold values from -0.21875 to 0.21875
- out_weight: bfloat16 [384, 768], replicated, may hold values from -0.3125 to 0.3125
- logit_scale: float32 [6], replicated, may hold values from 1 to 3
- grad_out: bfloat16 [64, 32, 32, 768], P('tm', 'lat', 'lon'), may hold values from -12 to 12
Outputs:
- grad_tokens: bfloat16 [64, 32, 32, 768], P('tm', 'lat', 'lon')
The draws below stay inside these ranges and needn't reach their ends.
All inputs are finite; a program needn't handle non-finite values.
Results may differ from the reference program's by a relative error of at most 0.012.
The reference program's roundings to bfloat16 on the way count: a program that leaves them out, or rounds other values in their place, can miss the bound.
Values may be sent and summed in bfloat16 or wider, within the bound.
A program may use at most 128 MiB of HBM per device.

```python
import math
import jax
import jax.numpy as jnp
from jax import lax

D = 768
HEADS = 6
HEAD_DIM = 64
BLOCK = 4
NT = 64
NH = 32
NW = 32


def draw_tokens(key, part):
    key_mine = jax.random.fold_in(key, 11)
    key_base = jax.random.fold_in(key_mine, 0)
    grid_shape = (NT, NH, NW, D)
    normal = jax.random.truncated_normal(key_base, -6.0, 6.0, grid_shape, jnp.float32)
    return normal.astype(jnp.bfloat16)


def draw_grad_out(key, part):
    key_mine = jax.random.fold_in(key, 23)
    key_base = jax.random.fold_in(key_mine, 0)
    grid_shape = (NT, NH, NW, D)
    normal = jax.random.truncated_normal(key_base, -6.0, 6.0, grid_shape, jnp.float32)
    return normal.astype(jnp.bfloat16)


def plant(array, stream_key, low, top_value):
    spot = [jax.random.randint(jax.random.fold_in(stream_key, axis), (), 0, length) for axis, length in enumerate(array.shape)]
    main_axis = array.shape.index(max(array.shape))
    neighbour = spot[:main_axis] + [(spot[main_axis] + 1) % array.shape[main_axis]] + spot[main_axis + 1:]
    return array.at[tuple(spot)].set(low).at[tuple(neighbour)].set(top_value)


def normal_values(rng, shape, width, reach, held_as=jnp.bfloat16):
    values = jax.random.normal(rng, shape, jnp.float32) * width
    return jnp.minimum(jnp.maximum(values, -reach), reach).astype(held_as)


def setup_inputs(seed: int = 0) -> dict:
    streams_of = jax.random.split(jax.random.key(seed), 8)
    tokens = draw_tokens(jax.random.fold_in(streams_of[7], 71), 0)
    key_count = plant(jax.random.randint(streams_of[1], (NT // BLOCK, NH // BLOCK, NW // BLOCK), 1, BLOCK**3 + 1), jax.random.fold_in(streams_of[1], 1), 1, BLOCK**3).astype(jnp.int32)
    norm_gain = jnp.clip(1.0 + 0.18 * jax.random.normal(streams_of[2], (D,), jnp.float32), 0.1, 1.9)
    qkv_weight = normal_values(streams_of[3], (3, D, HEADS * HEAD_DIM), D ** -0.5, 0.21875)
    out_weight = normal_values(streams_of[4], (HEADS * HEAD_DIM, D), (HEADS * HEAD_DIM) ** -0.5, 0.3125)
    logit_scale = jnp.clip(jnp.exp(jax.random.uniform(streams_of[5], (HEADS,), jnp.float32, math.log(1.0), math.log(3.0))), 1.0, 3.0)
    grad_out = draw_grad_out(jax.random.fold_in(streams_of[7], 71), 0)
    return dict(tokens=tokens, key_count=key_count, norm_gain=norm_gain, qkv_weight=qkv_weight, out_weight=out_weight, logit_scale=logit_scale, grad_out=grad_out)


EPS = 1e-06

def unit_rows(values):
    inverse = lax.rsqrt(lax.optimization_barrier(jnp.mean(values * values, -1, keepdims=True)) + EPS)
    return (values * inverse, inverse)

def unit_rows_back(values, inverse, grad_in):
    inner_mean = lax.optimization_barrier(jnp.mean(values * grad_in, -1, keepdims=True))
    return inverse * grad_in - inverse * inverse * inverse * values * inner_mean

def to_blocks(layout):
    shape_in = layout.shape
    trailing = shape_in[3:]
    split_up = layout.reshape((shape_in[0] // BLOCK, BLOCK, shape_in[1] // BLOCK, BLOCK, shape_in[2] // BLOCK, BLOCK) + trailing)
    axes_order = (0, 2, 4, 1, 3, 5) + tuple(range(6, 6 + len(trailing)))
    return split_up.transpose(axes_order).reshape((shape_in[0] // BLOCK, shape_in[1] // BLOCK, shape_in[2] // BLOCK, BLOCK * BLOCK * BLOCK) + trailing)

def from_blocks(blocked):
    shape_in = blocked.shape
    trailing = shape_in[4:]
    split_up = blocked.reshape(shape_in[:3] + (BLOCK, BLOCK, BLOCK) + trailing)
    axes_order = (0, 3, 1, 4, 2, 5) + tuple(range(6, 6 + len(trailing)))
    return split_up.transpose(axes_order).reshape((shape_in[0] * BLOCK, shape_in[1] * BLOCK, shape_in[2] * BLOCK) + trailing)

def gather_neighbours(blocked):
    inner_dims = (blocked.shape[0] - 2, blocked.shape[1] - 2, blocked.shape[2] - 2)
    pieces = []
    for frame_off in range(3):
        for row_off in range(3):
            for col_off in range(3):
                pieces.append(blocked[frame_off:frame_off + inner_dims[0], row_off:row_off + inner_dims[1], col_off:col_off + inner_dims[2]])
    stacked = jnp.stack(pieces, 3)
    return stacked.reshape((inner_dims[0] * inner_dims[1] * inner_dims[2], 27 * stacked.shape[4]) + stacked.shape[5:])

def spread_neighbours(nearby, inner_dims):
    trailing = nearby.shape[2:]
    block_cells = BLOCK * BLOCK * BLOCK
    blocked = nearby.reshape(inner_dims + (27, block_cells) + trailing)
    padded = jnp.zeros((inner_dims[0] + 2, inner_dims[1] + 2, inner_dims[2] + 2, block_cells) + trailing, nearby.dtype)
    offset_id = 0
    for frame_off in range(3):
        for row_off in range(3):
            for col_off in range(3):
                padded = padded.at[frame_off:frame_off + inner_dims[0], row_off:row_off + inner_dims[1], col_off:col_off + inner_dims[2]].add(blocked[:, :, :, offset_id])
                offset_id = offset_id + 1
    return padded

def query_side(query_blocks, keys_near, values_near, live_near, grad_blocks, scale_rows):
    scores = jnp.einsum('nqhe,nkhe->nhqk', query_blocks.astype(jnp.float32), keys_near.astype(jnp.float32)) * scale_rows[:, None, None]
    masked = jnp.exp(scores) * live_near[:, None, None, :]
    totals = lax.optimization_barrier(jnp.sum(masked, -1))
    prob_full = masked / totals[..., None]
    prob_half = prob_full.astype(jnp.bfloat16)
    attended = jnp.einsum('nhqk,nkhe->nqhe', prob_half.astype(jnp.float32), values_near.astype(jnp.float32))
    inner_grad = lax.optimization_barrier(jnp.sum(grad_blocks.astype(jnp.float32) * attended, -1))
    grad_prob = jnp.einsum('nqhe,nkhe->nhqk', grad_blocks.astype(jnp.float32), values_near.astype(jnp.float32))
    grad_score = (prob_full * (grad_prob - jnp.swapaxes(inner_grad, 1, 2)[..., None]) * scale_rows[:, None, None]).astype(jnp.bfloat16)
    grad_query = jnp.einsum('nhqk,nkhe->nqhe', grad_score.astype(jnp.float32), keys_near.astype(jnp.float32))
    return (prob_half, grad_score, grad_query, totals, inner_grad)

def pad_grid(layout):
    widths = [(BLOCK, BLOCK), (BLOCK, BLOCK), (0, 0)] + [(0, 0)] * (layout.ndim - 3)
    padded = jnp.pad(layout, widths)
    return jnp.concatenate([padded[:, :, -BLOCK:], padded, padded[:, :, :BLOCK]], 2)

def reference(tokens, key_count, norm_gain, qkv_weight, out_weight, logit_scale, grad_out):
    head_width = HEADS * HEAD_DIM
    grid_shape = (NT, NH, NW)
    heads_shape = grid_shape + (HEADS, HEAD_DIM)
    block_cells = BLOCK * BLOCK * BLOCK
    near_count = 27 * block_cells
    slab_grid = (1, NH // BLOCK, NW // BLOCK)
    slab_total = slab_grid[1] * slab_grid[2]
    scale_rows = logit_scale * (1.0 / math.sqrt(HEAD_DIM))
    token_values = tokens.astype(jnp.float32)
    normed_unit, row_inverse = unit_rows(token_values)
    normed = (normed_unit * norm_gain).astype(jnp.bfloat16)
    flat_normed = normed.reshape(NT * NH * NW, D)
    query_raw = jnp.dot(flat_normed, qkv_weight[0], preferred_element_type=jnp.float32).reshape(heads_shape)
    key_raw = jnp.dot(flat_normed, qkv_weight[1], preferred_element_type=jnp.float32).reshape(heads_shape)
    value_raw = jnp.dot(flat_normed, qkv_weight[2], preferred_element_type=jnp.float32)
    query_unit, query_inverse = unit_rows(query_raw)
    key_unit, key_inverse = unit_rows(key_raw)
    queries = query_unit.astype(jnp.bfloat16).reshape(grid_shape + (head_width,))
    keys_all = key_unit.astype(jnp.bfloat16).reshape(grid_shape + (head_width,))
    values_all = value_raw.astype(jnp.bfloat16).reshape(grid_shape + (head_width,))
    grad_attended = jnp.dot(grad_out.reshape(NT * NH * NW, D), out_weight.T, preferred_element_type=jnp.float32).astype(jnp.bfloat16).reshape(grid_shape + (head_width,))
    count_cells = jnp.repeat(jnp.repeat(jnp.repeat(key_count, BLOCK, 0), BLOCK, 1), BLOCK, 2)
    frame_pos = jnp.arange(NT, dtype=jnp.int32) % BLOCK
    row_pos = jnp.arange(NH, dtype=jnp.int32) % BLOCK
    col_pos = jnp.arange(NW, dtype=jnp.int32) % BLOCK
    position = (frame_pos[:, None, None] * BLOCK + row_pos[None, :, None]) * BLOCK + col_pos[None, None, :]
    live_all = (position < count_cells).astype(jnp.float32)
    kv_padded = pad_grid(jnp.stack([keys_all, values_all], 3))
    live_padded = pad_grid(live_all)

    def one_slab(pair_total, slab_id):
        start_row = (slab_id * BLOCK).astype(jnp.int32)
        kv_slab = lax.dynamic_slice_in_dim(kv_padded, start_row, 3 * BLOCK, 0)
        live_slab = lax.dynamic_slice_in_dim(live_padded, start_row, 3 * BLOCK, 0)
        query_slab = lax.dynamic_slice_in_dim(queries, start_row, BLOCK, 0)
        grad_slab = lax.dynamic_slice_in_dim(grad_attended, start_row, BLOCK, 0)
        kv_near = gather_neighbours(to_blocks(kv_slab))
        keys_near = kv_near[:, :, 0].reshape(slab_total, near_count, HEADS, HEAD_DIM)
        values_near = kv_near[:, :, 1].reshape(slab_total, near_count, HEADS, HEAD_DIM)
        live_near = gather_neighbours(to_blocks(live_slab))
        query_blocks = to_blocks(query_slab).reshape(slab_total, block_cells, HEADS, HEAD_DIM)
        grad_blocks = to_blocks(grad_slab).reshape(slab_total, block_cells, HEADS, HEAD_DIM)
        prob_half, grad_score, grad_query, totals, inner_grad = query_side(query_blocks, keys_near, values_near, live_near, grad_blocks, scale_rows)
        key_grad_near = jnp.einsum('nhqk,nqhe->nkhe', grad_score.astype(jnp.float32), query_blocks.astype(jnp.float32))
        value_grad_near = jnp.einsum('nhqk,nqhe->nkhe', prob_half.astype(jnp.float32), grad_blocks.astype(jnp.float32))
        pair_near = jnp.stack([key_grad_near.reshape(slab_total, near_count, head_width), value_grad_near.reshape(slab_total, near_count, head_width)], 2)
        pair_slab = from_blocks(spread_neighbours(pair_near, slab_grid))
        current = lax.dynamic_slice_in_dim(pair_total, start_row, 3 * BLOCK, 0)
        pair_total = lax.dynamic_update_slice_in_dim(pair_total, current + pair_slab, start_row, 0)
        query_grad = from_blocks(grad_query.reshape(slab_grid + (block_cells, head_width)))
        return (pair_total, query_grad)
    pair_init = jnp.zeros((NT + 2 * BLOCK, NH + 2 * BLOCK, NW + 2 * BLOCK, 2, head_width), jnp.float32)
    pair_padded, query_grads = lax.scan(one_slab, pair_init, jnp.arange(NT // BLOCK, dtype=jnp.int32))
    query_grad_all = query_grads.reshape(grid_shape + (head_width,))
    own_part = pair_padded[BLOCK:-BLOCK, BLOCK:-BLOCK]
    pair_grad = own_part[:, :, BLOCK:-BLOCK]
    pair_grad = pair_grad.at[:, :, :BLOCK].add(own_part[:, :, -BLOCK:])
    pair_grad = pair_grad.at[:, :, -BLOCK:].add(own_part[:, :, :BLOCK])
    key_grad = pair_grad[:, :, :, 0]
    value_grad = pair_grad[:, :, :, 1]
    query_grad_raw = unit_rows_back(query_raw, query_inverse, query_grad_all.reshape(heads_shape))
    key_grad_raw = unit_rows_back(key_raw, key_inverse, key_grad.reshape(heads_shape))
    grad_projected = jnp.stack([query_grad_raw.reshape(grid_shape + (head_width,)), key_grad_raw.reshape(grid_shape + (head_width,)), value_grad], 0).astype(jnp.bfloat16)
    flat_grad = grad_projected.reshape(3, NT * NH * NW, head_width)
    grad_normed = jnp.dot(flat_grad[0], qkv_weight[0].T, preferred_element_type=jnp.float32)
    grad_normed = grad_normed + jnp.dot(flat_grad[1], qkv_weight[1].T, preferred_element_type=jnp.float32)
    grad_normed = grad_normed + jnp.dot(flat_grad[2], qkv_weight[2].T, preferred_element_type=jnp.float32)
    grad_normed = grad_normed.reshape(grid_shape + (D,))
    grad_tokens = unit_rows_back(token_values, row_inverse, norm_gain * grad_normed)
    return grad_tokens.astype(jnp.bfloat16)
```

```python
import functools
import math

import jax
import jax.numpy as jnp
from jax import lax
from jax.experimental import pallas as pl
from jax.experimental.pallas import tpu as pltpu
from jax.sharding import PartitionSpec as P

MESH = pl.DeviceIdType.MESH
F32 = jnp.float32
BF16 = jnp.bfloat16
HEADS = 6
HEAD_DIM = 64
WIDTH = HEADS * HEAD_DIM
CELLS = 64
EPS = 1e-6
DEAD = 64.0
HIGH = lax.Precision.HIGHEST


def nt(a, b):
    return lax.dot_general(a, b, (((1,), (1,)), ((), ())), preferred_element_type=F32)


def tn(a, b):
    return lax.dot_general(a, b, (((0,), (0,)), ((), ())), preferred_element_type=F32)


def nn(a, b, precision=None):
    return lax.dot_general(
        a, b, (((1,), (0,)), ((), ())), precision=precision, preferred_element_type=F32
    )


def iota(shape, dim):
    return lax.broadcasted_iota(jnp.int32, shape, dim)


def original_row(p):
    return (
        (((p >> 4) & 3) << 5) + (((p >> 2) & 3) << 3) + (((p >> 6) & 1) << 2) + (p & 3)
    )


def head_mean():
    shape = (WIDTH, WIDTH)
    return jnp.where(
        iota(shape, 0) // HEAD_DIM == iota(shape, 1) // HEAD_DIM, 1.0 / HEAD_DIM, 0.0
    ).astype(F32)


def kernel(
    nt_size, nx, nl,
    count, logit, tok, gain, wqkv, wout, gout, out,
    kv, ee, dd, gs, acc, rz, xs, rx, ys, ry, bdq, bdo, tot, dlt, dq,
    xp_s, raw_s, rows_s,
    fs, fr, bs, br,
):
    tm = lax.axis_index("tm")
    lat = lax.axis_index("lat")
    lon = lax.axis_index("lon")
    x, yh = lat // 2, lat % 2
    y = yh * nl + lon
    ny = 2 * nl

    def ydev(k):
        yy = (y + k + ny) % ny
        return (tm, x * 2 + yy // nl, yy % nl)

    def xdev(k):
        return (tm, ((x + k + nx) % nx) * 2 + yh, lon)

    def tdev(k):
        return ((tm + k + nt_size) % nt_size, lat, lon)

    far_fwd = 1 - 2 * yh
    barrier = pltpu.get_barrier_semaphore()
    for dev in (ydev(1), ydev(-1), ydev(nl - 1), ydev(1 - nl), xdev(1), xdev(-1), tdev(1), tdev(-1)):
        pl.semaphore_signal(barrier, inc=1, device_id=dev, device_id_type=MESH)

    shape2 = (128, 128)
    perm = (iota(shape2, 1) == original_row(iota(shape2, 0))).astype(F32).astype(BF16)
    tok_flat = tok[...].astype(F32).reshape(128, 768).astype(BF16)
    go_flat = gout[...].astype(F32).reshape(128, 768).astype(BF16)
    xp = nn(perm, tok_flat)
    xp_s[...] = xp
    row_inv = lax.rsqrt(jnp.mean(xp * xp, -1, keepdims=True) + EPS)
    rows_s[...] = jnp.broadcast_to(row_inv, (128, 128))
    normed = (xp * row_inv * gain[...]).astype(BF16)
    q_raw = nn(normed, wqkv[0])
    k_raw = nn(normed, wqkv[1])
    v_bf = nn(normed, wqkv[2]).astype(BF16)
    raw_s[0] = q_raw
    raw_s[1] = k_raw
    mean_mat = head_mean()
    q_inv = lax.rsqrt(nn(q_raw * q_raw, mean_mat, HIGH) + EPS)
    k_inv = lax.rsqrt(nn(k_raw * k_raw, mean_mat, HIGH) + EPS)
    raw_s[2] = q_inv
    raw_s[3] = k_inv
    row1 = iota((128, 1), 0)
    limit = jnp.where(row1 < CELLS, count[0, 0, 0], count[0, 0, 1])
    live = (row1 & (CELLS - 1)) < limit
    k_bf = jnp.where(live, k_raw * k_inv, DEAD).astype(BF16)
    kv[1, 0, :, 0:WIDTH] = k_bf[:CELLS]
    kv[1, 1, :, 0:WIDTH] = k_bf[CELLS:]
    kv[1, 0, :, WIDTH:] = v_bf[:CELLS]
    kv[1, 1, :, WIDTH:] = v_bf[CELLS:]

    def remote(src, dst, send, recv, dev):
        return pltpu.make_async_remote_copy(
            src_ref=src, dst_ref=dst, send_sem=send, recv_sem=recv,
            device_id=dev, device_id_type=MESH,
        )

    def fwd(src_slot, dst_slot, dev):
        remote(
            kv.at[1, src_slot], kv.at[1, dst_slot],
            fs.at[dst_slot - 2], fr.at[dst_slot - 2], dev,
        ).start()

    def fwd_z(slot):
        remote(kv.at[1, slot], kv.at[0, slot], fs.at[10 + slot], fr.at[10 + slot], tdev(1)).start()
        remote(kv.at[1, slot], kv.at[2, slot], fs.at[22 + slot], fr.at[22 + slot], tdev(-1)).start()

    pl.semaphore_wait(barrier, 8)
    fwd(1, 2, ydev(1))
    fwd(0, 3, ydev(-1))

    q_f = q_raw * q_inv
    go_p = nn(perm, go_flat).astype(BF16)
    ga = nt(go_p, wout[...]).astype(BF16).astype(F32)
    low_lane = iota((128, 128), 1) < HEAD_DIM
    for i in range(3):
        qc = q_f[:, 128 * i : 128 * i + 128]
        gc = ga[:, 128 * i : 128 * i + 128]
        bdq[i, 0:128] = jnp.where(low_lane, qc, 0.0).astype(BF16)
        bdq[i, 128:256] = jnp.where(low_lane, 0.0, qc).astype(BF16)
        bdo[i, 0:128] = jnp.where(low_lane, gc, 0.0).astype(BF16)
        bdo[i, 128:256] = jnp.where(low_lane, 0.0, gc).astype(BF16)
    tot[...] = jnp.zeros_like(tot)
    dlt[...] = jnp.zeros_like(dlt)
    dq[...] = jnp.zeros_like(dq)

    lane2 = iota((1, 256), 1)
    scales = [
        jnp.where(lane2 < 128, logit[2 * i], logit[2 * i + 1]) * (1.0 / math.sqrt(HEAD_DIM))
        for i in range(3)
    ]
    edge = jnp.where(
        (iota((128, 256), 0) >= CELLS) == ((iota((128, 256), 1) & 127) >= CELLS), 1.0, 0.0
    )
    far_ok = jnp.where((lat + 2 * yh - 1 + far_fwd * 0 >= 0) & (lat + 2 * yh - 1 < 2 * nx), 1.0, 0.0)
    before_ok = jnp.where(tm > 0, 1.0, 0.0)
    after_ok = jnp.where(tm < nt_size - 1, 1.0, 0.0)
    plane_ok = (before_ok, 1.0, after_ok)

    def pass1(p, g):
        is_far = jnp.where(g >= 4, 1.0, 0.0)
        ok = plane_ok[p] * (1.0 - is_far * (1.0 - far_ok))
        odd = (g % 2).astype(F32)
        bound = (1.0 - odd * (1.0 - edge)) * (ok * 64.0) - 32.0
        mask = None
        for i in range(3):
            keys = kv[p, pl.ds(2 * g, 2), :, 128 * i : 128 * i + 128].reshape(128, 128)
            vals = kv[p, pl.ds(2 * g, 2), :, WIDTH + 128 * i : WIDTH + 128 * i + 128].reshape(128, 128)
            if mask is None:
                mask = keys[:, 0:1].astype(F32) < bound
            s = nt(keys, bdq[i])
            e = jnp.where(mask, jnp.exp(s * scales[i]), 0.0)
            d = nt(vals, bdo[i])
            lanes = slice(256 * i, 256 * i + 256)
            ee[p, g, :, lanes] = e
            dd[p, g, :, lanes] = d
            tot[:, lanes] += jnp.sum(e.reshape(16, 8, 256), 0)
            dlt[:, lanes] += jnp.sum((e * d).reshape(16, 8, 256), 0)

    slot_left = 2 + 4 * ((lon + nl - 1) // nl)
    slot_right = 7 - 4 * ((lon + 1) // nl)

    def wait_fwd(j, dst):
        remote(dst, dst, fs.at[j], fr.at[j], tdev(1)).wait_recv()

    def gather_step(g, carry):
        @pl.when(g < 6)
        def _():
            @pl.when(g >= 1)
            def _():
                wait_fwd(2 * g - 2, kv.at[1, 2 * g])
                wait_fwd(2 * g - 1, kv.at[1, 2 * g + 1])

            @pl.when(g == 1)
            def _():
                fwd(2, 4, ydev(nl - 1))
                fwd(3, 5, ydev(1 - nl))

            @pl.when(g == 2)
            def _():
                fwd(4, 6, ydev(1))
                fwd(5, 7, ydev(-1))
                fwd(5, 8, xdev(far_fwd))
                fwd(4, 9, xdev(far_fwd))

            @pl.when(g == 3)
            def _():
                fwd(slot_left, 10, xdev(far_fwd))
                fwd(slot_right, 11, xdev(far_fwd))

            fwd_z(2 * g)
            fwd_z(2 * g + 1)
            pass1(1, g)

        @pl.when(g >= 1)
        def _():
            h = g - 1
            for j in range(2):
                wait_fwd(10 + 2 * h + j, kv.at[0, 2 * h + j])
                wait_fwd(22 + 2 * h + j, kv.at[2, 2 * h + j])
            pass1(0, h)
            pass1(2, h)

        return carry

    lax.fori_loop(0, 7, gather_step, 0)

    inv_rows, dlt_rows = [], []
    for i in range(3):
        lanes = slice(256 * i, 256 * i + 256)
        inv = 1.0 / jnp.sum(tot[:, lanes], 0, keepdims=True)
        inv_rows.append(inv)
        dlt_rows.append(jnp.sum(dlt[:, lanes], 0, keepdims=True) * inv)

    def pass2(p, g):
        for i in range(3):
            lanes = slice(256 * i, 256 * i + 256)
            keys = kv[p, pl.ds(2 * g, 2), :, 128 * i : 128 * i + 128].reshape(128, 128)
            pr = ee[p, g, :, lanes] * inv_rows[i]
            ds = (pr * (dd[p, g, :, lanes] - dlt_rows[i]) * scales[i]).astype(BF16)
            dk = nn(ds, bdq[i]).reshape(2, CELLS, 128)
            dv = nn(pr.astype(BF16), bdo[i]).reshape(2, CELLS, 128)
            dq[i] += tn(ds, keys)
            klanes = slice(128 * i, 128 * i + 128)
            vlanes = slice(WIDTH + 128 * i, WIDTH + 128 * i + 128)
            if p == 1:
                acc[pl.ds(2 * g, 2), :, klanes] = dk
                acc[pl.ds(2 * g, 2), :, vlanes] = dv
            else:
                gs[p // 2, pl.ds(2 * g, 2), :, klanes] = dk.astype(BF16)
                gs[p // 2, pl.ds(2 * g, 2), :, vlanes] = dv.astype(BF16)

    def back_z(slot):
        remote(gs.at[0, slot], rz.at[0, slot], bs.at[10 + slot], br.at[10 + slot], tdev(-1)).start()
        remote(gs.at[1, slot], rz.at[1, slot], bs.at[22 + slot], br.at[22 + slot], tdev(1)).start()

    def wait_back(j, dst):
        remote(dst, dst, bs.at[j], br.at[j], tdev(1)).wait_recv()

    def back_x(slot):
        xs[slot - 8] = acc[slot].astype(BF16)
        remote(
            xs.at[slot - 8], rx.at[slot - 8], bs.at[slot - 2], br.at[slot - 2], xdev(-far_fwd)
        ).start()

    def back_y(slot, dev):
        ys[slot - 2] = acc[slot].astype(BF16)
        remote(ys.at[slot - 2], ry.at[slot - 2], bs.at[slot - 2], br.at[slot - 2], dev).start()

    def take_x(slot, into):
        wait_back(slot - 2, rx.at[slot - 8])
        acc[into] += rx[slot - 8].astype(F32)

    def take_y(slot, into):
        wait_back(slot - 2, ry.at[slot - 2])
        acc[into] += ry[slot - 2].astype(F32)

    def back_step(k, carry):
        @pl.when(k < 6)
        def _():
            g = 5 - k
            pass2(0, g)
            pass2(2, g)
            back_z(2 * g)
            back_z(2 * g + 1)
            pass2(1, g)

        @pl.when(k >= 2)
        def _():
            h = 7 - k
            for j in range(2):
                slot = 2 * h + j
                wait_back(10 + slot, rz.at[0, slot])
                wait_back(22 + slot, rz.at[1, slot])
                acc[slot] += rz[0, slot].astype(F32) + rz[1, slot].astype(F32)

            @pl.when(h == 5)
            def _():
                back_x(10)
                back_x(11)

            @pl.when(h == 4)
            def _():
                back_x(8)
                back_x(9)

            @pl.when(h == 3)
            def _():
                take_x(10, slot_left)
                take_x(11, slot_right)
                back_y(6, ydev(-1))
                back_y(7, ydev(1))

            @pl.when(h == 2)
            def _():
                take_x(8, 5)
                take_x(9, 4)
                take_y(6, 4)
                take_y(7, 5)
                back_y(4, ydev(1 - nl))
                back_y(5, ydev(nl - 1))

            @pl.when(h == 1)
            def _():
                take_y(4, 2)
                take_y(5, 3)
                back_y(2, ydev(-1))
                back_y(3, ydev(1))

            @pl.when(h == 0)
            def _():
                take_y(2, 1)
                take_y(3, 0)

        return carry

    lax.fori_loop(0, 8, back_step, 0)

    def drain(j, carry):
        remote(kv.at[1, 0], kv.at[1, 0], fs.at[j], fr.at[j], tdev(1)).wait_send()
        remote(ys.at[0], ry.at[0], bs.at[j], br.at[j], tdev(1)).wait_send()
        return carry

    lax.fori_loop(0, 34, drain, 0)

    mean_mat = head_mean()

    def rows_back(raw, inverse, grad):
        return inverse * grad - inverse * inverse * inverse * raw * nn(raw * grad, mean_mat, HIGH)

    dq_full = jnp.concatenate(
        [jnp.where(low_lane, dq[i, 0:128], dq[i, 128:256]) for i in range(3)], axis=1
    )
    pair = acc[0:2].reshape(128, 2 * WIDTH)
    gq = rows_back(raw_s[0], raw_s[2], dq_full).astype(BF16)
    gk = rows_back(raw_s[1], raw_s[3], pair[:, :WIDTH]).astype(BF16)
    gv = pair[:, WIDTH:].astype(BF16)
    gn = nt(gq, wqkv[0]) + nt(gk, wqkv[1]) + nt(gv, wqkv[2])
    g = gain[...] * gn
    xv = xp_s[...]
    r = rows_s[:, 0:1]
    res = r * g - r * r * r * xv * jnp.mean(xv * g, -1, keepdims=True)
    perm_back = (iota(shape2, 0) == original_row(iota(shape2, 1))).astype(F32).astype(BF16)
    out[...] = nn(perm_back, res.astype(BF16)).reshape(4, 4, 8, 768).astype(BF16)


def solution(mesh):
    nt_size, nlat, nl = mesh.shape["tm"], mesh.shape["lat"], mesh.shape["lon"]

    def per_device(tokens, key_count, norm_gain, qkv_weight, out_weight, logit_scale, grad_out):
        vmem = pl.BlockSpec(memory_space=pltpu.VMEM)
        smem = pl.BlockSpec(memory_space=pltpu.SMEM)
        block = (CELLS, 2 * WIDTH)
        return pl.pallas_call(
            functools.partial(kernel, nt_size, nlat // 2, nl),
            out_shape=jax.ShapeDtypeStruct(tokens.shape, BF16),
            in_specs=[smem, smem, vmem, vmem, vmem, vmem, vmem],
            out_specs=vmem,
            scratch_shapes=[
                pltpu.VMEM((3, 12) + block, BF16),
                pltpu.VMEM((3, 6, 128, 768), F32),
                pltpu.VMEM((3, 6, 128, 768), F32),
                pltpu.VMEM((2, 12) + block, BF16),
                pltpu.VMEM((12,) + block, F32),
                pltpu.VMEM((2, 12) + block, BF16),
                pltpu.VMEM((4,) + block, BF16),
                pltpu.VMEM((4,) + block, BF16),
                pltpu.VMEM((6,) + block, BF16),
                pltpu.VMEM((6,) + block, BF16),
                pltpu.VMEM((3, 256, 128), BF16),
                pltpu.VMEM((3, 256, 128), BF16),
                pltpu.VMEM((8, 768), F32),
                pltpu.VMEM((8, 768), F32),
                pltpu.VMEM((3, 256, 128), F32),
                pltpu.VMEM((128, 768), F32),
                pltpu.VMEM((4, 128, WIDTH), F32),
                pltpu.VMEM((128, 128), F32),
                pltpu.SemaphoreType.DMA((34,)),
                pltpu.SemaphoreType.DMA((34,)),
                pltpu.SemaphoreType.DMA((34,)),
                pltpu.SemaphoreType.DMA((34,)),
            ],
            compiler_params=pltpu.CompilerParams(
                collective_id=0, has_side_effects=True, vmem_limit_bytes=56 * 1024 * 1024
            ),
        )(
            key_count, logit_scale, tokens, norm_gain.reshape(1, -1), qkv_weight, out_weight,
            grad_out,
        )

    split = P("tm", "lat", "lon", None)
    return jax.shard_map(
        per_device,
        mesh=mesh,
        in_specs=(split, P("tm", "lat", "lon"), P(), P(), P(), P(), split),
        out_specs=split,
        check_vma=False,
    )
```

```python
import functools
import math

import jax
import jax.numpy as jnp
from jax import lax
from jax.experimental import pallas as pl
from jax.experimental.pallas import tpu as pltpu
from jax.sharding import PartitionSpec as P

MESH = pl.DeviceIdType.MESH
F32 = jnp.float32
BF16 = jnp.bfloat16
HEADS = 6
HEAD_DIM = 64
WIDTH = HEADS * HEAD_DIM
CELLS = 64
EPS = 1e-6
DEAD = 64.0
CHUNKS = 2
ROWS = CELLS // CHUNKS


def nt(a, b):
    return lax.dot_general(a, b, (((1,), (1,)), ((), ())), preferred_element_type=F32)


def tn(a, b):
    return lax.dot_general(a, b, (((0,), (0,)), ((), ())), preferred_element_type=F32)


def nn(a, b):
    return lax.dot_general(a, b, (((1,), (0,)), ((), ())), preferred_element_type=F32)


def nn_split(a, b):
    high = a.astype(BF16)
    return nn(high, b) + nn((a - high.astype(F32)).astype(BF16), b)


def iota(shape, dim):
    return lax.broadcasted_iota(jnp.int32, shape, dim)


def original_row(p):
    return (
        (((p >> 4) & 3) << 5) + (((p >> 2) & 3) << 3) + (((p >> 6) & 1) << 2) + (p & 3)
    )


def head_mean():
    shape = (WIDTH, WIDTH)
    return jnp.where(
        iota(shape, 0) // HEAD_DIM == iota(shape, 1) // HEAD_DIM, 1.0 / HEAD_DIM, 0.0
    ).astype(BF16)


def kernel(
    nt_size, nx, nl,
    count, logit, gain, tok_h, w_h, wout_h, gout_h, out,
    kv, ee, dd, gs, acc, rz, xs, rx, ys, ry, bdq, bdo, tot, dlt, dq,
    xp_s, raw_s, rows_s, tok, wqkv, wout, gout,
    fs, fr, bs, br, ins,
):
    tm = lax.axis_index("tm")
    lat = lax.axis_index("lat")
    lon = lax.axis_index("lon")
    x, yh = lat // 2, lat % 2
    y = yh * nl + lon
    ny = 2 * nl

    def ydev(k):
        yy = (y + k + ny) % ny
        return (tm, x * 2 + yy // nl, yy % nl)

    def xdev(k):
        return (tm, (x + k) * 2 + yh, lon)

    def tdev(k):
        return (tm + k, lat, lon)

    far_fwd = 1 - 2 * yh
    has_lo, has_hi = tm > 0, tm < nt_size - 1
    x_lo, x_hi = x > 0, x < nx - 1
    x_to = ((yh == 0) & x_hi) | ((yh == 1) & x_lo)
    x_from = ((yh == 0) & x_lo) | ((yh == 1) & x_hi)

    barrier = pltpu.get_barrier_semaphore()

    def greet(dev):
        pl.semaphore_signal(barrier, inc=1, device_id=dev, device_id_type=MESH)

    for k in (1, -1, nl - 1, 1 - nl):
        greet(ydev(k))
    for there, dev in ((x_lo, xdev(-1)), (x_hi, xdev(1)), (has_lo, tdev(-1)), (has_hi, tdev(1))):
        pl.when(there)(functools.partial(greet, dev))
    greeted = (
        4 + jnp.minimum(x, 1) + jnp.minimum(nx - 1 - x, 1)
        + jnp.minimum(tm, 1) + jnp.minimum(nt_size - 1 - tm, 1)
    )

    loads = [
        pltpu.make_async_copy(src, dst, ins.at[n])
        for n, (src, dst) in enumerate((
            (tok_h, tok), (w_h.at[1], wqkv.at[1]), (w_h.at[2], wqkv.at[2]),
            (w_h.at[0], wqkv.at[0]), (gout_h, gout), (wout_h, wout),
        ))
    ]
    for load in loads:
        load.start()

    shape2 = (128, 128)
    perm = (iota(shape2, 1) == original_row(iota(shape2, 0))).astype(F32).astype(BF16)
    mean_mat = head_mean()
    loads[0].wait()
    xp = nn(perm, tok[...].astype(F32).reshape(128, 768).astype(BF16))
    row_inv = lax.rsqrt(jnp.mean(xp * xp, -1, keepdims=True) + EPS)
    normed = (xp * row_inv * gain[...][None, :]).astype(BF16)
    loads[1].wait()
    k_raw = nn(normed, wqkv[1])
    k_inv = lax.rsqrt(nn_split(k_raw * k_raw, mean_mat) + EPS)
    loads[2].wait()
    v_bf = nn(normed, wqkv[2]).astype(BF16)
    row1 = iota((128, 1), 0)
    limit = jnp.where(row1 < CELLS, count[0, 0, 0], count[0, 0, 1])
    live = (row1 & (CELLS - 1)) < limit
    k_bf = jnp.where(live, k_raw * k_inv, DEAD).astype(BF16)
    kv[1, 0, :, 0:WIDTH] = k_bf[:CELLS]
    kv[1, 1, :, 0:WIDTH] = k_bf[CELLS:]
    kv[1, 0, :, WIDTH:] = v_bf[:CELLS]
    kv[1, 1, :, WIDTH:] = v_bf[CELLS:]

    def piece(ref, index, c):
        return ref.at[index + (pl.ds(ROWS * c, ROWS),)]

    def remote(src, dst, send, recv, dev):
        return pltpu.make_async_remote_copy(
            src_ref=src, dst_ref=dst, send_sem=send, recv_sem=recv,
            device_id=dev, device_id_type=MESH,
        )

    def fwd(src_slot, dst_slot, c, dev):
        j = (dst_slot - 2) * CHUNKS + c
        remote(
            piece(kv, (1, src_slot), c), piece(kv, (1, dst_slot), c), fs.at[j], fr.at[j], dev
        ).start()

    def fwd_z(slot, c):
        lo, hi = (10 + slot) * CHUNKS + c, (22 + slot) * CHUNKS + c
        src = piece(kv, (1, slot), c)

        @pl.when(has_hi)
        def _():
            remote(src, piece(kv, (0, slot), c), fs.at[lo], fr.at[lo], tdev(1)).start()

        @pl.when(has_lo)
        def _():
            remote(src, piece(kv, (2, slot), c), fs.at[hi], fr.at[hi], tdev(-1)).start()

    pl.semaphore_wait(barrier, greeted)
    for c in range(CHUNKS):
        fwd(1, 2, c, ydev(1 - nl))
        fwd(0, 3, c, ydev(nl - 1))
    for c in range(CHUNKS):
        fwd(1, 4, c, ydev(1))
        fwd(0, 5, c, ydev(-1))
    for c in range(CHUNKS):
        fwd_z(0, c)
        fwd_z(1, c)

    xp_s[...] = xp
    rows_s[...] = jnp.broadcast_to(row_inv, (128, 128))
    loads[3].wait()
    q_raw = nn(normed, wqkv[0])
    q_inv = lax.rsqrt(nn_split(q_raw * q_raw, mean_mat) + EPS)
    raw_s[0] = q_raw
    raw_s[1] = k_raw
    raw_s[2] = q_inv
    raw_s[3] = k_inv
    q_f = q_raw * q_inv
    loads[4].wait()
    go_p = nn(perm, gout[...].astype(F32).reshape(128, 768).astype(BF16)).astype(BF16)
    loads[5].wait()
    ga = nt(go_p, wout[...]).astype(BF16).astype(F32)
    low_lane = iota((128, 128), 1) < HEAD_DIM
    for i in range(3):
        qc = q_f[:, 128 * i : 128 * i + 128]
        gc = ga[:, 128 * i : 128 * i + 128]
        bdq[i, 0:128] = jnp.where(low_lane, qc, 0.0).astype(BF16)
        bdq[i, 128:256] = jnp.where(low_lane, 0.0, qc).astype(BF16)
        bdo[i, 0:128] = jnp.where(low_lane, gc, 0.0).astype(BF16)
        bdo[i, 128:256] = jnp.where(low_lane, 0.0, gc).astype(BF16)
    tot[...] = jnp.zeros_like(tot)
    dlt[...] = jnp.zeros_like(dlt)
    dq[...] = jnp.zeros_like(dq)

    lane2 = iota((1, 256), 1)
    scales = [
        jnp.where(lane2 < 128, logit[2 * i], logit[2 * i + 1]) * (1.0 / math.sqrt(HEAD_DIM))
        for i in range(3)
    ]
    edge = jnp.where(
        (iota((128, 256), 0) >= CELLS) == ((iota((128, 256), 1) & 127) >= CELLS), 1.0, 0.0
    )

    def pass1(p, g):
        sided = jnp.where((g == 1) | (g == 2) | (g == 4), 1.0, 0.0)
        bound = (1.0 - sided * (1.0 - edge)) * 64.0 - 32.0
        mask = None
        for i in range(3):
            keys = kv[p, pl.ds(2 * g, 2), :, 128 * i : 128 * i + 128].reshape(128, 128)
            vals = kv[p, pl.ds(2 * g, 2), :, WIDTH + 128 * i : WIDTH + 128 * i + 128].reshape(128, 128)
            if mask is None:
                mask = keys[:, 0:1].astype(F32) < bound
            s = nt(keys, bdq[i])
            e = jnp.where(mask, jnp.exp(s * scales[i]), 0.0)
            d = nt(vals, bdo[i])
            lanes = slice(256 * i, 256 * i + 256)
            ee[p, g, :, lanes] = e
            dd[p, g, :, lanes] = d
            tot[:, lanes] += jnp.sum(e.reshape(16, 8, 256), 0)
            dlt[:, lanes] += jnp.sum((e * d).reshape(16, 8, 256), 0)

    def here(g):
        return (g < 4) | x_from

    def wait_fwd(first, p, slot, c):
        j = (first + slot) * CHUNKS + c
        dst = piece(kv, (p, slot), c)
        remote(dst, dst, fs.at[j], fr.at[j], ydev(1)).wait_recv()

    def gather_step(g, carry):
        @pl.when((g < 6) & here(g))
        def _():
            for c in range(CHUNKS):
                @pl.when(g >= 1)
                def _(c=c):
                    wait_fwd(-2, 1, 2 * g, c)
                    wait_fwd(-2, 1, 2 * g + 1, c)

                @pl.when(g == 1)
                def _(c=c):
                    fwd(2, 6, c, ydev(-1))
                    fwd(3, 7, c, ydev(1))

                    @pl.when(x_to & (lon > 0))
                    def _():
                        fwd(2, 8, c, xdev(far_fwd))

                    @pl.when(x_to & (lon < nl - 1))
                    def _():
                        fwd(3, 9, c, xdev(far_fwd))

                @pl.when((g == 2) & x_to)
                def _(c=c):
                    @pl.when(lon == 0)
                    def _():
                        fwd(4, 8, c, xdev(far_fwd))

                    @pl.when(lon == nl - 1)
                    def _():
                        fwd(5, 9, c, xdev(far_fwd))

                @pl.when((g == 3) & x_to)
                def _(c=c):
                    fwd(7, 10, c, xdev(far_fwd))
                    fwd(6, 11, c, xdev(far_fwd))

                @pl.when(g >= 1)
                def _(c=c):
                    fwd_z(2 * g, c)
                    fwd_z(2 * g + 1, c)

            pass1(1, g)

        @pl.when((g >= 2) & here(g - 2))
        def _():
            h = g - 2

            @pl.when(has_lo)
            def _():
                for j in range(2):
                    for c in range(CHUNKS):
                        wait_fwd(10, 0, 2 * h + j, c)
                pass1(0, h)

            @pl.when(has_hi)
            def _():
                for j in range(2):
                    for c in range(CHUNKS):
                        wait_fwd(22, 2, 2 * h + j, c)
                pass1(2, h)

        return carry

    lax.fori_loop(0, 8, gather_step, 0)

    inv_rows, dlt_rows = [], []
    for i in range(3):
        lanes = slice(256 * i, 256 * i + 256)
        inv = 1.0 / jnp.sum(tot[:, lanes], 0, keepdims=True)
        inv_rows.append(inv)
        dlt_rows.append(jnp.sum(dlt[:, lanes], 0, keepdims=True) * inv)

    def pass2(p, g):
        for i in range(3):
            lanes = slice(256 * i, 256 * i + 256)
            keys = kv[p, pl.ds(2 * g, 2), :, 128 * i : 128 * i + 128].reshape(128, 128)
            pr = ee[p, g, :, lanes] * inv_rows[i]
            ds = (pr * (dd[p, g, :, lanes] - dlt_rows[i]) * scales[i]).astype(BF16)
            dk = nn(ds, bdq[i]).reshape(2, CELLS, 128)
            dv = nn(pr.astype(BF16), bdo[i]).reshape(2, CELLS, 128)
            dq[i] += tn(ds, keys)
            klanes = slice(128 * i, 128 * i + 128)
            vlanes = slice(WIDTH + 128 * i, WIDTH + 128 * i + 128)
            if p == 1:
                acc[pl.ds(2 * g, 2), :, klanes] = dk
                acc[pl.ds(2 * g, 2), :, vlanes] = dv
            else:
                gs[p // 2, pl.ds(2 * g, 2), :, klanes] = dk.astype(BF16)
                gs[p // 2, pl.ds(2 * g, 2), :, vlanes] = dv.astype(BF16)

    def back_z(slot, c):
        lo, hi = (10 + slot) * CHUNKS + c, (22 + slot) * CHUNKS + c

        @pl.when(has_lo)
        def _():
            remote(
                piece(gs, (0, slot), c), piece(rz, (0, slot), c), bs.at[lo], br.at[lo], tdev(-1)
            ).start()

        @pl.when(has_hi)
        def _():
            remote(
                piece(gs, (1, slot), c), piece(rz, (1, slot), c), bs.at[hi], br.at[hi], tdev(1)
            ).start()

    def wait_back(j, dst):
        remote(dst, dst, bs.at[j], br.at[j], ydev(1)).wait_recv()

    def rows_of(c):
        return pl.ds(ROWS * c, ROWS)

    def take_z(slot, c):
        @pl.when(has_hi)
        def _():
            wait_back((10 + slot) * CHUNKS + c, piece(rz, (0, slot), c))
            acc[slot, rows_of(c)] += rz[0, slot, rows_of(c)].astype(F32)

        @pl.when(has_lo)
        def _():
            wait_back((22 + slot) * CHUNKS + c, piece(rz, (1, slot), c))
            acc[slot, rows_of(c)] += rz[1, slot, rows_of(c)].astype(F32)

    def back(slot, base, sends, lands, c, dev):
        j = (slot - 2) * CHUNKS + c
        sends[slot - base, rows_of(c)] = acc[slot, rows_of(c)].astype(BF16)
        remote(
            piece(sends, (slot - base,), c), piece(lands, (slot - base,), c), bs.at[j], br.at[j], dev
        ).start()

    def take(slot, base, lands, c, into):
        wait_back((slot - 2) * CHUNKS + c, piece(lands, (slot - base,), c))
        acc[into, rows_of(c)] += lands[slot - base, rows_of(c)].astype(F32)

    def back_x(slot, c):
        back(slot, 8, xs, rx, c, xdev(-far_fwd))

    def take_x(slot, c, into):
        take(slot, 8, rx, c, into)

    def back_y(slot, c, dev):
        back(slot, 2, ys, ry, c, dev)

    def take_y(slot, c, into):
        take(slot, 2, ry, c, into)

    def back_step(k, carry):
        @pl.when((k < 6) & here(5 - k))
        def _():
            g = 5 - k

            @pl.when(has_lo)
            def _():
                pass2(0, g)

            @pl.when(has_hi)
            def _():
                pass2(2, g)

            for c in range(CHUNKS):
                if c > 0:
                    @pl.when(k == 1)
                    def _(c=c):
                        back_z(10, c)
                        back_z(11, c)

                @pl.when(k > (0 if c > 0 else -1))
                def _(c=c):
                    back_z(2 * g, c)
                    back_z(2 * g + 1, c)

            pass2(1, g)

        @pl.when((k == 2) & x_from)
        def _():
            for c in range(CHUNKS):
                for slot in (10, 11, 8, 9):
                    take_z(slot, c)
                    back_x(slot, c)

        @pl.when(k >= 3)
        def _():
            h = 6 - k
            for c in range(CHUNKS):
                take_z(2 * h, c)
                take_z(2 * h + 1, c)

                @pl.when(h == 3)
                def _(c=c):
                    @pl.when(x_to)
                    def _():
                        take_x(10, c, 7)
                        take_x(11, c, 6)
                    back_y(6, c, ydev(1))
                    back_y(7, c, ydev(-1))

                @pl.when(h == 2)
                def _(c=c):
                    @pl.when(x_to & (lon == 0))
                    def _():
                        take_x(8, c, 4)

                    @pl.when(x_to & (lon == nl - 1))
                    def _():
                        take_x(9, c, 5)
                    back_y(4, c, ydev(-1))
                    back_y(5, c, ydev(1))

                @pl.when(h == 1)
                def _(c=c):
                    @pl.when(x_to & (lon > 0))
                    def _():
                        take_x(8, c, 2)

                    @pl.when(x_to & (lon < nl - 1))
                    def _():
                        take_x(9, c, 3)
                    take_y(6, c, 2)
                    take_y(7, c, 3)
                    back_y(2, c, ydev(nl - 1))
                    back_y(3, c, ydev(1 - nl))

                @pl.when(h == 0)
                def _(c=c):
                    take_y(4, c, 1)
                    take_y(5, c, 0)
                    take_y(2, c, 1)
                    take_y(3, c, 0)

        return carry

    lax.fori_loop(0, 7, back_step, 0)

    def drain(sems, first, slots):
        def one(j, carry):
            whole = piece(ys, (0,), 0)
            remote(whole, whole, sems.at[j], sems.at[j], ydev(1)).wait_send()
            return carry

        lax.fori_loop(first * CHUNKS, (first + slots) * CHUNKS, one, 0)

    drain(fs, 0, 6)
    drain(bs, 0, 6)
    pl.when(x_to)(functools.partial(drain, fs, 6, 4))
    pl.when(x_from)(functools.partial(drain, bs, 6, 4))
    for sems, first, there in (
        (fs, 10, has_hi), (fs, 22, has_lo), (bs, 10, has_lo), (bs, 22, has_hi)
    ):
        pl.when(there)(functools.partial(drain, sems, first, 8))
        pl.when(there & x_from)(functools.partial(drain, sems, first + 8, 4))

    def rows_back(raw, inverse, grad):
        return inverse * grad - inverse * inverse * inverse * raw * nn_split(raw * grad, mean_mat)

    dq_full = jnp.concatenate(
        [jnp.where(low_lane, dq[i, 0:128], dq[i, 128:256]) for i in range(3)], axis=1
    )
    pair = acc[0:2].reshape(128, 2 * WIDTH)
    gq = rows_back(raw_s[0], raw_s[2], dq_full).astype(BF16)
    gk = rows_back(raw_s[1], raw_s[3], pair[:, :WIDTH]).astype(BF16)
    gv = pair[:, WIDTH:].astype(BF16)
    gn = nt(gq, wqkv[0]) + nt(gk, wqkv[1]) + nt(gv, wqkv[2])
    g = gain[...][None, :] * gn
    xv = xp_s[...]
    r = rows_s[:, 0:1]
    res = r * g - r * r * r * xv * jnp.mean(xv * g, -1, keepdims=True)
    perm_back = (iota(shape2, 0) == original_row(iota(shape2, 1))).astype(F32).astype(BF16)
    out[...] = nn(perm_back, res.astype(BF16)).reshape(4, 4, 8, 768).astype(BF16)


def solution(mesh):
    nt_size, nlat, nl = mesh.shape["tm"], mesh.shape["lat"], mesh.shape["lon"]

    def per_device(tokens, key_count, norm_gain, qkv_weight, out_weight, logit_scale, grad_out):
        vmem = pl.BlockSpec(memory_space=pltpu.VMEM)
        smem = pl.BlockSpec(memory_space=pltpu.SMEM)
        hbm = pl.BlockSpec(memory_space=pl.ANY)
        block = (CELLS, 2 * WIDTH)
        return pl.pallas_call(
            functools.partial(kernel, nt_size, nlat // 2, nl),
            out_shape=jax.ShapeDtypeStruct(tokens.shape, BF16),
            in_specs=[smem, smem, vmem, hbm, hbm, hbm, hbm],
            out_specs=vmem,
            scratch_shapes=[
                pltpu.VMEM((3, 12) + block, BF16),
                pltpu.VMEM((3, 6, 128, 768), F32),
                pltpu.VMEM((3, 6, 128, 768), F32),
                pltpu.VMEM((2, 12) + block, BF16),
                pltpu.VMEM((12,) + block, F32),
                pltpu.VMEM((2, 12) + block, BF16),
                pltpu.VMEM((4,) + block, BF16),
                pltpu.VMEM((4,) + block, BF16),
                pltpu.VMEM((6,) + block, BF16),
                pltpu.VMEM((6,) + block, BF16),
                pltpu.VMEM((3, 256, 128), BF16),
                pltpu.VMEM((3, 256, 128), BF16),
                pltpu.VMEM((8, 768), F32),
                pltpu.VMEM((8, 768), F32),
                pltpu.VMEM((3, 256, 128), F32),
                pltpu.VMEM((128, 768), F32),
                pltpu.VMEM((4, 128, WIDTH), F32),
                pltpu.VMEM((128, 128), F32),
                pltpu.VMEM(tokens.shape, BF16),
                pltpu.VMEM(qkv_weight.shape, BF16),
                pltpu.VMEM(out_weight.shape, BF16),
                pltpu.VMEM(grad_out.shape, BF16),
                pltpu.SemaphoreType.DMA((34 * CHUNKS,)),
                pltpu.SemaphoreType.DMA((34 * CHUNKS,)),
                pltpu.SemaphoreType.DMA((34 * CHUNKS,)),
                pltpu.SemaphoreType.DMA((34 * CHUNKS,)),
                pltpu.SemaphoreType.DMA((6,)),
            ],
            compiler_params=pltpu.CompilerParams(
                collective_id=0, has_side_effects=True, vmem_limit_bytes=56 * 1024 * 1024
            ),
        )(
            key_count, logit_scale, norm_gain, tokens, qkv_weight, out_weight, grad_out,
        )

    split = P("tm", "lat", "lon", None)
    return jax.shard_map(
        per_device,
        mesh=mesh,
        in_specs=(split, P("tm", "lat", "lon"), P(), P(), P(), P(), split),
        out_specs=split,
        check_vma=False,
    )
```

```python
import functools
import math

import jax
import jax.numpy as jnp
from jax import lax
from jax.experimental import pallas as pl
from jax.experimental.pallas import tpu as pltpu
from jax.sharding import PartitionSpec as P

MESH = pl.DeviceIdType.MESH
F32 = jnp.float32
BF16 = jnp.bfloat16
HEADS = 6
HEAD_DIM = 64
WIDTH = HEADS * HEAD_DIM
CELLS = 64
EPS = 1e-6
DEAD = 64.0
CHUNKS = 2
ROWS = CELLS // CHUNKS


def nt(a, b):
    return lax.dot_general(a, b, (((1,), (1,)), ((), ())), preferred_element_type=F32)


def tn(a, b):
    return lax.dot_general(a, b, (((0,), (0,)), ((), ())), preferred_element_type=F32)


def nn(a, b):
    return lax.dot_general(a, b, (((1,), (0,)), ((), ())), preferred_element_type=F32)


def nn_split(a, b):
    high = a.astype(BF16)
    return nn(high, b) + nn((a - high.astype(F32)).astype(BF16), b)


def iota(shape, dim):
    return lax.broadcasted_iota(jnp.int32, shape, dim)


def original_row(p):
    return (
        (((p >> 4) & 3) << 5) + (((p >> 2) & 3) << 3) + (((p >> 6) & 1) << 2) + (p & 3)
    )


def head_mean():
    shape = (WIDTH, WIDTH)
    return jnp.where(
        (iota(shape, 0) >> 6) == (iota(shape, 1) >> 6), 1.0 / HEAD_DIM, 0.0
    ).astype(BF16)


def kernel(
    nt_size, nx, nl,
    count, logit, gain, tok_h, w_h, wout_h, gout_h, out,
    kv, ee, dd, gs, acc, rz, xs, rx, ys, ry, bdq, bdo, tot, dlt, dq,
    xp_s, raw_s, rows_s, tok, wqkv, wout, gout,
    fs, fr, bs, br, ins,
):
    tm = lax.axis_index("tm")
    lat = lax.axis_index("lat")
    lon = lax.axis_index("lon")
    x, yh = lat // 2, lat % 2
    y = yh * nl + lon
    ny = 2 * nl

    def ydev(k):
        yy = (y + k + ny) % ny
        return (tm, x * 2 + yy // nl, yy % nl)

    def xdev(k):
        return (tm, (x + k) * 2 + yh, lon)

    def tdev(k):
        return (tm + k, lat, lon)

    far_fwd = 1 - 2 * yh
    has_lo, has_hi = tm > 0, tm < nt_size - 1
    x_lo, x_hi = x > 0, x < nx - 1
    x_to = ((yh == 0) & x_hi) | ((yh == 1) & x_lo)
    x_from = ((yh == 0) & x_lo) | ((yh == 1) & x_hi)

    barrier = pltpu.get_barrier_semaphore()

    def greet(dev):
        pl.semaphore_signal(barrier, inc=1, device_id=dev, device_id_type=MESH)

    for k in (1, -1, nl - 1, 1 - nl):
        greet(ydev(k))
    for there, dev in ((x_lo, xdev(-1)), (x_hi, xdev(1)), (has_lo, tdev(-1)), (has_hi, tdev(1))):
        pl.when(there)(functools.partial(greet, dev))
    greeted = (
        4 + jnp.minimum(x, 1) + jnp.minimum(nx - 1 - x, 1)
        + jnp.minimum(tm, 1) + jnp.minimum(nt_size - 1 - tm, 1)
    )

    loads = [
        pltpu.make_async_copy(src, dst, ins.at[n])
        for n, (src, dst) in enumerate((
            (tok_h, tok), (w_h.at[1], wqkv.at[1]), (w_h.at[2], wqkv.at[2]),
            (w_h.at[0], wqkv.at[0]), (gout_h, gout), (wout_h, wout),
        ))
    ]
    for load in loads[:3]:
        load.start()

    shape2 = (128, 128)
    perm = (iota(shape2, 1) == original_row(iota(shape2, 0))).astype(F32).astype(BF16)
    mean_mat = head_mean()
    loads[0].wait()
    xp = nn(perm, tok[...].astype(F32).reshape(128, 768).astype(BF16))
    row_inv = lax.rsqrt(jnp.mean(xp * xp, -1, keepdims=True) + EPS)
    normed = (xp * row_inv * gain[...][None, :]).astype(BF16)
    loads[1].wait()
    for load in loads[3:]:
        load.start()
    k_raw = nn(normed, wqkv[1])
    k_inv = lax.rsqrt(nn_split(k_raw * k_raw, mean_mat) + EPS)
    loads[2].wait()
    v_bf = nn(normed, wqkv[2]).astype(BF16)
    row1 = iota((128, 1), 0)
    limit = jnp.where(row1 < CELLS, count[0, 0, 0], count[0, 0, 1])
    live = (row1 & (CELLS - 1)) < limit
    k_bf = jnp.where(live, k_raw * k_inv, DEAD).astype(BF16)
    kv[1, 0, :, 0:WIDTH] = k_bf[:CELLS]
    kv[1, 1, :, 0:WIDTH] = k_bf[CELLS:]
    kv[1, 0, :, WIDTH:] = v_bf[:CELLS]
    kv[1, 1, :, WIDTH:] = v_bf[CELLS:]

    def piece(ref, index, c):
        return ref.at[index + (pl.ds(ROWS * c, ROWS),)]

    def remote(src, dst, send, recv, dev):
        return pltpu.make_async_remote_copy(
            src_ref=src, dst_ref=dst, send_sem=send, recv_sem=recv,
            device_id=dev, device_id_type=MESH,
        )

    def fwd(src_slot, dst_slot, c, dev):
        j = (dst_slot - 2) * CHUNKS + c
        remote(
            piece(kv, (1, src_slot), c), piece(kv, (1, dst_slot), c), fs.at[j], fr.at[j], dev
        ).start()

    def pair(ref, index, first, c):
        return ref.at[index + (pl.ds(first, 2), pl.ds(ROWS * c, ROWS))]

    def fwd_mid(c, dev):
        j = 8 * CHUNKS + c
        remote(
            pair(kv, (1,), 6, c), pair(kv, (1,), 10, c), fs.at[j], fr.at[j], dev
        ).start()

    def fwd_z(g, c):
        lo, hi = (9 + g) * CHUNKS + c, (15 + g) * CHUNKS + c
        src = pair(kv, (1,), 2 * g, c)

        @pl.when(has_hi)
        def _():
            remote(src, pair(kv, (0,), 2 * g, c), fs.at[lo], fr.at[lo], tdev(1)).start()

        @pl.when(has_lo)
        def _():
            remote(src, pair(kv, (2,), 2 * g, c), fs.at[hi], fr.at[hi], tdev(-1)).start()

    pl.semaphore_wait(barrier, greeted)
    for c in range(CHUNKS):
        fwd(1, 2, c, ydev(1 - nl))
        fwd(0, 3, c, ydev(nl - 1))
    for c in range(CHUNKS):
        fwd(1, 4, c, ydev(1))
        fwd(0, 5, c, ydev(-1))
    for c in range(CHUNKS):
        fwd_z(0, c)

    xp_s[...] = xp
    rows_s[...] = jnp.broadcast_to(row_inv, (128, 128))
    loads[3].wait()
    q_raw = nn(normed, wqkv[0])
    q_inv = lax.rsqrt(nn_split(q_raw * q_raw, mean_mat) + EPS)
    raw_s[0] = q_raw
    raw_s[1] = k_raw
    raw_s[2] = q_inv
    raw_s[3] = k_inv
    q_f = q_raw * q_inv
    loads[4].wait()
    go_p = nn(perm, gout[...].astype(F32).reshape(128, 768).astype(BF16)).astype(BF16)
    loads[5].wait()
    ga = nt(go_p, wout[...]).astype(BF16).astype(F32)
    low_lane = iota((128, 128), 1) < HEAD_DIM
    for i in range(3):
        qc = q_f[:, 128 * i : 128 * i + 128]
        gc = ga[:, 128 * i : 128 * i + 128]
        bdq[i, 0:128] = jnp.where(low_lane, qc, 0.0).astype(BF16)
        bdq[i, 128:256] = jnp.where(low_lane, 0.0, qc).astype(BF16)
        bdo[i, 0:128] = jnp.where(low_lane, gc, 0.0).astype(BF16)
        bdo[i, 128:256] = jnp.where(low_lane, 0.0, gc).astype(BF16)
    tot[...] = jnp.zeros_like(tot)
    dlt[...] = jnp.zeros_like(dlt)
    dq[...] = jnp.zeros_like(dq)

    lane2 = iota((1, 256), 1)
    scales = [
        jnp.where(lane2 < 128, logit[2 * i], logit[2 * i + 1]) * (1.0 / math.sqrt(HEAD_DIM))
        for i in range(3)
    ]
    edge = jnp.where(
        (iota((128, 256), 0) >= CELLS) == ((iota((128, 256), 1) & 127) >= CELLS), 1.0, 0.0
    )

    def pass1(p, g):
        sided = jnp.where((g == 1) | (g == 2) | (g == 4), 1.0, 0.0)
        bound = (1.0 - sided * (1.0 - edge)) * 64.0 - 32.0
        mask = None
        for i in range(3):
            keys = kv[p, pl.ds(2 * g, 2), :, 128 * i : 128 * i + 128].reshape(128, 128)
            vals = kv[p, pl.ds(2 * g, 2), :, WIDTH + 128 * i : WIDTH + 128 * i + 128].reshape(128, 128)
            if mask is None:
                mask = keys[:, 0:1].astype(F32) < bound
            s = nt(keys, bdq[i])
            e = jnp.where(mask, jnp.exp(s * scales[i]), 0.0)
            d = nt(vals, bdo[i])
            lanes = slice(256 * i, 256 * i + 256)
            ee[p, g, :, lanes] = e
            dd[p, g, :, lanes] = d
            tot[:, lanes] += jnp.sum(e.reshape(16, 8, 256), 0)
            dlt[:, lanes] += jnp.sum((e * d).reshape(16, 8, 256), 0)

    def here(g):
        return (g < 4) | x_from

    def wait_fwd(slot, c):
        j = (slot - 2) * CHUNKS + c
        dst = piece(kv, (1, slot), c)
        remote(dst, dst, fs.at[j], fr.at[j], ydev(1)).wait_recv()

    def wait_pair(first, p, g, c):
        j = first * CHUNKS + c
        dst = pair(kv, (p,), 2 * g, c)
        remote(dst, dst, fs.at[j], fr.at[j], ydev(1)).wait_recv()

    def gather_step(g, carry):
        @pl.when((g < 6) & here(g))
        def _():
            for c in range(CHUNKS):
                @pl.when((g >= 1) & (g < 5))
                def _(c=c):
                    wait_fwd(2 * g, c)
                    wait_fwd(2 * g + 1, c)

                @pl.when(g == 5)
                def _(c=c):
                    wait_pair(8, 1, 5, c)

                @pl.when(g == 1)
                def _(c=c):
                    fwd(2, 6, c, ydev(-1))
                    fwd(3, 7, c, ydev(1))

                    @pl.when(x_to & (lon > 0))
                    def _():
                        fwd(2, 8, c, xdev(far_fwd))

                    @pl.when(x_to & (lon < nl - 1))
                    def _():
                        fwd(3, 9, c, xdev(far_fwd))

                @pl.when((g == 2) & x_to)
                def _(c=c):
                    @pl.when(lon == 0)
                    def _():
                        fwd(4, 8, c, xdev(far_fwd))

                    @pl.when(lon == nl - 1)
                    def _():
                        fwd(5, 9, c, xdev(far_fwd))

                @pl.when((g == 3) & x_to)
                def _(c=c):
                    fwd_mid(c, xdev(far_fwd))

                @pl.when(g >= 1)
                def _(c=c):
                    fwd_z(g, c)

            pass1(1, g)

        @pl.when((g >= 2) & here(g - 2))
        def _():
            h = g - 2

            @pl.when(has_lo)
            def _():
                for c in range(CHUNKS):
                    wait_pair(9 + h, 0, h, c)
                pass1(0, h)

            @pl.when(has_hi)
            def _():
                for c in range(CHUNKS):
                    wait_pair(15 + h, 2, h, c)
                pass1(2, h)

        return carry

    lax.fori_loop(0, 8, gather_step, 0)

    inv_rows, dlt_rows = [], []
    for i in range(3):
        lanes = slice(256 * i, 256 * i + 256)
        inv = 1.0 / jnp.sum(tot[:, lanes], 0, keepdims=True)
        inv_rows.append(inv)
        dlt_rows.append(jnp.sum(dlt[:, lanes], 0, keepdims=True) * inv)

    def pass2(p, g):
        for i in range(3):
            lanes = slice(256 * i, 256 * i + 256)
            keys = kv[p, pl.ds(2 * g, 2), :, 128 * i : 128 * i + 128].reshape(128, 128)
            pr = ee[p, g, :, lanes] * inv_rows[i]
            ds = (pr * (dd[p, g, :, lanes] - dlt_rows[i]) * scales[i]).astype(BF16)
            dk = nn(ds, bdq[i]).reshape(2, CELLS, 128)
            dv = nn(pr.astype(BF16), bdo[i]).reshape(2, CELLS, 128)
            dq[i] += tn(ds, keys)
            klanes = slice(128 * i, 128 * i + 128)
            vlanes = slice(WIDTH + 128 * i, WIDTH + 128 * i + 128)
            if p == 1:
                acc[pl.ds(2 * g, 2), :, klanes] = dk
                acc[pl.ds(2 * g, 2), :, vlanes] = dv
            else:
                gs[p // 2, pl.ds(2 * g, 2), :, klanes] = dk.astype(BF16)
                gs[p // 2, pl.ds(2 * g, 2), :, vlanes] = dv.astype(BF16)

    def back_z(g, c):
        lo, hi = (9 + g) * CHUNKS + c, (15 + g) * CHUNKS + c

        @pl.when(has_lo)
        def _():
            remote(
                pair(gs, (0,), 2 * g, c), pair(rz, (0,), 2 * g, c), bs.at[lo], br.at[lo], tdev(-1)
            ).start()

        @pl.when(has_hi)
        def _():
            remote(
                pair(gs, (1,), 2 * g, c), pair(rz, (1,), 2 * g, c), bs.at[hi], br.at[hi], tdev(1)
            ).start()

    def wait_back(j, dst):
        remote(dst, dst, bs.at[j], br.at[j], ydev(1)).wait_recv()

    def rows_of(c):
        return pl.ds(ROWS * c, ROWS)

    def take_z(g, c):
        slots = pl.ds(2 * g, 2)

        @pl.when(has_hi)
        def _():
            wait_back((9 + g) * CHUNKS + c, pair(rz, (0,), 2 * g, c))
            acc[slots, rows_of(c)] += rz[0, slots, rows_of(c)].astype(F32)

        @pl.when(has_lo)
        def _():
            wait_back((15 + g) * CHUNKS + c, pair(rz, (1,), 2 * g, c))
            acc[slots, rows_of(c)] += rz[1, slots, rows_of(c)].astype(F32)

    def back(slot, base, sends, lands, c, dev):
        j = (slot - 2) * CHUNKS + c
        sends[slot - base, rows_of(c)] = acc[slot, rows_of(c)].astype(BF16)
        remote(
            piece(sends, (slot - base,), c), piece(lands, (slot - base,), c), bs.at[j], br.at[j], dev
        ).start()

    def take(slot, base, lands, c, into):
        wait_back((slot - 2) * CHUNKS + c, piece(lands, (slot - base,), c))
        acc[into, rows_of(c)] += lands[slot - base, rows_of(c)].astype(F32)

    def back_x(slot, c):
        back(slot, 8, xs, rx, c, xdev(-far_fwd))

    def take_x(slot, c, into):
        take(slot, 8, rx, c, into)

    def back_y(slot, c, dev):
        back(slot, 2, ys, ry, c, dev)

    def take_y(slot, c, into):
        take(slot, 2, ry, c, into)

    def back_mid(c):
        j = 8 * CHUNKS + c
        xs[2:4, rows_of(c)] = acc[10:12, rows_of(c)].astype(BF16)
        remote(
            pair(xs, (), 2, c), pair(rx, (), 2, c), bs.at[j], br.at[j], xdev(-far_fwd)
        ).start()

    def take_mid(c):
        wait_back(8 * CHUNKS + c, pair(rx, (), 2, c))
        acc[6:8, rows_of(c)] += rx[2:4, rows_of(c)].astype(F32)

    def far_back(c):
        take_z(5, c)
        back_mid(c)
        take_z(4, c)
        back_x(8, c)
        back_x(9, c)

    def back_step(k, carry):
        g = 5 - k + jnp.where(k == 4, 1, 0) - jnp.where(k == 3, 1, 0)

        @pl.when(here(g))
        def _():
            @pl.when(has_lo)
            def _():
                pass2(0, g)

            @pl.when(has_hi)
            def _():
                pass2(2, g)

            for c in range(CHUNKS):
                if c > 0:
                    @pl.when(k == 1)
                    def _(c=c):
                        back_z(5, c)

                @pl.when(k > (0 if c > 0 else -1))
                def _(c=c):
                    back_z(g, c)

            pass2(1, g)

        @pl.when((k == 3) & x_from)
        def _():
            far_back(0)

        return carry

    lax.fori_loop(0, 6, back_step, 0)

    def drain(sems, first, count, whole):
        def one(j, carry):
            remote(whole, whole, sems.at[j], sems.at[j], ydev(1)).wait_send()
            return carry

        lax.fori_loop(first * CHUNKS, (first + count) * CHUNKS, one, 0)

    one_piece, two_pieces = piece(ys, (0,), 0), pair(gs, (0,), 0, 0)
    x_left, x_right = x_to & (lon > 0), x_to & (lon < nl - 1)
    x_left_end, x_right_end = x_to & (lon == 0), x_to & (lon == nl - 1)

    @pl.when(x_from)
    def _():
        for c in range(1, CHUNKS):
            far_back(c)

    for c in range(CHUNKS):
        take_z(3, c)
        pl.when(x_to)(functools.partial(take_mid, c))
        back_y(6, c, ydev(1))
        back_y(7, c, ydev(-1))

    def send_a5(c):
        take_z(1, c)
        pl.when(x_left)(functools.partial(take_x, 8, c, 2))
        pl.when(x_right)(functools.partial(take_x, 9, c, 3))
        take_y(6, c, 2)
        take_y(7, c, 3)
        back_y(2, c, ydev(nl - 1))
        back_y(3, c, ydev(1 - nl))

    def send_a1(c):
        take_z(2, c)
        pl.when(x_left_end)(functools.partial(take_x, 8, c, 4))
        pl.when(x_right_end)(functools.partial(take_x, 9, c, 5))
        back_y(4, c, ydev(-1))
        back_y(5, c, ydev(1))

    send_a5(0)
    for c in range(CHUNKS):
        send_a1(c)
    for c in range(1, CHUNKS):
        send_a5(c)
    for c in range(CHUNKS):
        take_z(0, c)
    drain(fs, 0, 6, one_piece)

    @pl.when(x_to)
    def _():
        drain(fs, 6, 2, one_piece)
        drain(fs, 8, 1, two_pieces)

    @pl.when(x_from)
    def _():
        drain(bs, 6, 2, one_piece)
        drain(bs, 8, 1, two_pieces)

    for sems, first, there in (
        (fs, 9, has_hi), (fs, 15, has_lo), (bs, 9, has_lo), (bs, 15, has_hi)
    ):
        pl.when(there)(functools.partial(drain, sems, first, 4, two_pieces))
        pl.when(there & x_from)(functools.partial(drain, sems, first + 4, 2, two_pieces))

    for c in range(CHUNKS):
        take_y(4, c, 1)
        take_y(5, c, 0)
    for c in range(CHUNKS):
        take_y(2, c, 1)
        take_y(3, c, 0)
    drain(bs, 0, 6, one_piece)

    def rows_back(raw, inverse, grad):
        return inverse * grad - inverse * inverse * inverse * raw * nn_split(raw * grad, mean_mat)

    dq_full = jnp.concatenate(
        [jnp.where(low_lane, dq[i, 0:128], dq[i, 128:256]) for i in range(3)], axis=1
    )
    pair = acc[0:2].reshape(128, 2 * WIDTH)
    gq = rows_back(raw_s[0], raw_s[2], dq_full).astype(BF16)
    gk = rows_back(raw_s[1], raw_s[3], pair[:, :WIDTH]).astype(BF16)
    gv = pair[:, WIDTH:].astype(BF16)
    gn = nt(gq, wqkv[0]) + nt(gk, wqkv[1]) + nt(gv, wqkv[2])
    g = gain[...][None, :] * gn
    xv = xp_s[...]
    r = rows_s[:, 0:1]
    res = r * g - r * r * r * xv * jnp.mean(xv * g, -1, keepdims=True)
    perm_back = (iota(shape2, 0) == original_row(iota(shape2, 1))).astype(F32).astype(BF16)
    out[...] = nn(perm_back, res.astype(BF16)).reshape(4, 4, 8, 768).astype(BF16)


def solution(mesh):
    nt_size, nlat, nl = mesh.shape["tm"], mesh.shape["lat"], mesh.shape["lon"]

    def per_device(tokens, key_count, norm_gain, qkv_weight, out_weight, logit_scale, grad_out):
        vmem = pl.BlockSpec(memory_space=pltpu.VMEM)
        smem = pl.BlockSpec(memory_space=pltpu.SMEM)
        hbm = pl.BlockSpec(memory_space=pl.ANY)
        block = (CELLS, 2 * WIDTH)
        return pl.pallas_call(
            functools.partial(kernel, nt_size, nlat // 2, nl),
            out_shape=jax.ShapeDtypeStruct(tokens.shape, BF16),
            in_specs=[smem, smem, vmem, hbm, hbm, hbm, hbm],
            out_specs=vmem,
            scratch_shapes=[
                pltpu.VMEM((3, 12) + block, BF16),
                pltpu.VMEM((3, 6, 128, 768), F32),
                pltpu.VMEM((3, 6, 128, 768), F32),
                pltpu.VMEM((2, 12) + block, BF16),
                pltpu.VMEM((12,) + block, F32),
                pltpu.VMEM((2, 12) + block, BF16),
                pltpu.VMEM((4,) + block, BF16),
                pltpu.VMEM((4,) + block, BF16),
                pltpu.VMEM((6,) + block, BF16),
                pltpu.VMEM((6,) + block, BF16),
                pltpu.VMEM((3, 256, 128), BF16),
                pltpu.VMEM((3, 256, 128), BF16),
                pltpu.VMEM((8, 768), F32),
                pltpu.VMEM((8, 768), F32),
                pltpu.VMEM((3, 256, 128), F32),
                pltpu.VMEM((128, 768), F32),
                pltpu.VMEM((4, 128, WIDTH), F32),
                pltpu.VMEM((128, 128), F32),
                pltpu.VMEM(tokens.shape, BF16),
                pltpu.VMEM(qkv_weight.shape, BF16),
                pltpu.VMEM(out_weight.shape, BF16),
                pltpu.VMEM(grad_out.shape, BF16),
                pltpu.SemaphoreType.DMA((21 * CHUNKS,)),
                pltpu.SemaphoreType.DMA((21 * CHUNKS,)),
                pltpu.SemaphoreType.DMA((21 * CHUNKS,)),
                pltpu.SemaphoreType.DMA((21 * CHUNKS,)),
                pltpu.SemaphoreType.DMA((6,)),
            ],
            compiler_params=pltpu.CompilerParams(
                collective_id=0, has_side_effects=True, vmem_limit_bytes=56 * 1024 * 1024
            ),
        )(
            key_count, logit_scale, norm_gain, tokens, qkv_weight, out_weight, grad_out,
        )

    split = P("tm", "lat", "lon", None)
    return jax.shard_map(
        per_device,
        mesh=mesh,
        in_specs=(split, P("tm", "lat", "lon"), P(), P(), P(), P(), split),
        out_specs=split,
        check_vma=False,
    )
```

```python
import functools
import math

import jax
import jax.numpy as jnp
from jax import lax
from jax.experimental import pallas as pl
from jax.experimental.pallas import tpu as pltpu
from jax.sharding import PartitionSpec as P

MESH = pl.DeviceIdType.MESH
F32 = jnp.float32
BF16 = jnp.bfloat16
HEADS = 6
HEAD_DIM = 64
WIDTH = HEADS * HEAD_DIM
CELLS = 64
EPS = 1e-6
DEAD = 64.0
CHUNKS = 2
ROWS = CELLS // CHUNKS


def nt(a, b):
    return lax.dot_general(a, b, (((1,), (1,)), ((), ())), preferred_element_type=F32)


def tn(a, b):
    return lax.dot_general(a, b, (((0,), (0,)), ((), ())), preferred_element_type=F32)


def nn(a, b):
    return lax.dot_general(a, b, (((1,), (0,)), ((), ())), preferred_element_type=F32)


def nn_split(a, b):
    high = a.astype(BF16)
    return nn(high, b) + nn((a - high.astype(F32)).astype(BF16), b)


def iota(shape, dim):
    return lax.broadcasted_iota(jnp.int32, shape, dim)


def original_row(p):
    return (
        (((p >> 4) & 3) << 5) + (((p >> 2) & 3) << 3) + (((p >> 6) & 1) << 2) + (p & 3)
    )


def head_mean():
    shape = (WIDTH, WIDTH)
    return jnp.where(
        (iota(shape, 0) >> 6) == (iota(shape, 1) >> 6), 1.0 / HEAD_DIM, 0.0
    ).astype(BF16)


def kernel(
    nt_size, nx, nl,
    count, logit, gain, tok_h, w_h, wout_h, gout_h, out,
    kv, ee, dd, gs, acc, rz, xs, rx, ys, ry, bdq, bdo, tot, dlt, dq,
    xp_s, gn_q, raw_s, rows_s, tok, wqkv, wout, gout,
    fs, fr, bs, br, ins,
):
    tm = lax.axis_index("tm")
    lat = lax.axis_index("lat")
    lon = lax.axis_index("lon")
    x, yh = lat // 2, lat % 2
    y = yh * nl + lon
    ny = 2 * nl

    def ydev(k):
        yy = (y + k + ny) % ny
        return (tm, x * 2 + yy // nl, yy % nl)

    def xdev(k):
        return (tm, (x + k) * 2 + yh, lon)

    def tdev(k):
        return (tm + k, lat, lon)

    far_fwd = 1 - 2 * yh
    has_lo, has_hi = tm > 0, tm < nt_size - 1
    x_lo, x_hi = x > 0, x < nx - 1
    x_to = ((yh == 0) & x_hi) | ((yh == 1) & x_lo)
    x_from = ((yh == 0) & x_lo) | ((yh == 1) & x_hi)

    barrier = pltpu.get_barrier_semaphore()

    def greet(dev):
        pl.semaphore_signal(barrier, inc=1, device_id=dev, device_id_type=MESH)

    for k in (1, -1, nl - 1, 1 - nl):
        greet(ydev(k))
    for there, dev in ((x_lo, xdev(-1)), (x_hi, xdev(1)), (has_lo, tdev(-1)), (has_hi, tdev(1))):
        pl.when(there)(functools.partial(greet, dev))
    greeted = (
        4 + jnp.minimum(x, 1) + jnp.minimum(nx - 1 - x, 1)
        + jnp.minimum(tm, 1) + jnp.minimum(nt_size - 1 - tm, 1)
    )

    loads = [
        pltpu.make_async_copy(src, dst, ins.at[n])
        for n, (src, dst) in enumerate((
            (tok_h, tok), (w_h.at[1], wqkv.at[1]), (w_h.at[2], wqkv.at[2]),
            (w_h.at[0], wqkv.at[0]), (gout_h, gout), (wout_h, wout),
        ))
    ]
    for load in loads[:3]:
        load.start()

    shape2 = (128, 128)
    perm = (iota(shape2, 1) == original_row(iota(shape2, 0))).astype(F32).astype(BF16)
    mean_mat = head_mean()
    loads[0].wait()
    xp = nn(perm, tok[...].astype(F32).reshape(128, 768).astype(BF16))
    row_inv = lax.rsqrt(jnp.mean(xp * xp, -1, keepdims=True) + EPS)
    normed = (xp * row_inv * gain[...][None, :]).astype(BF16)
    loads[1].wait()
    for load in loads[3:]:
        load.start()
    k_raw = nn(normed, wqkv[1])
    k_inv = lax.rsqrt(nn_split(k_raw * k_raw, mean_mat) + EPS)
    loads[2].wait()
    v_bf = nn(normed, wqkv[2]).astype(BF16)
    row1 = iota((128, 1), 0)
    limit = jnp.where(row1 < CELLS, count[0, 0, 0], count[0, 0, 1])
    live = (row1 & (CELLS - 1)) < limit
    k_bf = jnp.where(live, k_raw * k_inv, DEAD).astype(BF16)
    kv[1, 0, :, 0:WIDTH] = k_bf[:CELLS]
    kv[1, 1, :, 0:WIDTH] = k_bf[CELLS:]
    kv[1, 0, :, WIDTH:] = v_bf[:CELLS]
    kv[1, 1, :, WIDTH:] = v_bf[CELLS:]

    def piece(ref, index, c):
        return ref.at[index + (pl.ds(ROWS * c, ROWS),)]

    def remote(src, dst, send, recv, dev):
        return pltpu.make_async_remote_copy(
            src_ref=src, dst_ref=dst, send_sem=send, recv_sem=recv,
            device_id=dev, device_id_type=MESH,
        )

    def fwd(src_slot, dst_slot, c, dev):
        j = (dst_slot - 2) * CHUNKS + c
        remote(
            piece(kv, (1, src_slot), c), piece(kv, (1, dst_slot), c), fs.at[j], fr.at[j], dev
        ).start()

    def pair(ref, index, first, c):
        return ref.at[index + (pl.ds(first, 2), pl.ds(ROWS * c, ROWS))]

    def fwd_mid(c, dev):
        j = 8 * CHUNKS + c
        remote(
            pair(kv, (1,), 6, c), pair(kv, (1,), 10, c), fs.at[j], fr.at[j], dev
        ).start()

    def fwd_z(g, c):
        lo, hi = (9 + g) * CHUNKS + c, (15 + g) * CHUNKS + c
        src = pair(kv, (1,), 2 * g, c)

        @pl.when(has_hi)
        def _():
            remote(src, pair(kv, (0,), 2 * g, c), fs.at[lo], fr.at[lo], tdev(1)).start()

        @pl.when(has_lo)
        def _():
            remote(src, pair(kv, (2,), 2 * g, c), fs.at[hi], fr.at[hi], tdev(-1)).start()

    pl.semaphore_wait(barrier, greeted)
    for c in range(CHUNKS):
        fwd(1, 2, c, ydev(1 - nl))
        fwd(0, 3, c, ydev(nl - 1))
    for c in range(CHUNKS):
        fwd(1, 4, c, ydev(1))
        fwd(0, 5, c, ydev(-1))
    for c in range(CHUNKS):
        fwd_z(0, c)

    xp_s[...] = xp
    rows_s[...] = jnp.broadcast_to(row_inv, (128, 128))
    loads[3].wait()
    q_raw = nn(normed, wqkv[0])
    q_inv = lax.rsqrt(nn_split(q_raw * q_raw, mean_mat) + EPS)
    raw_s[0] = q_raw
    raw_s[1] = k_raw
    raw_s[2] = q_inv
    raw_s[3] = k_inv
    q_f = q_raw * q_inv
    loads[4].wait()
    go_p = nn(perm, gout[...].astype(F32).reshape(128, 768).astype(BF16)).astype(BF16)
    loads[5].wait()
    ga = nt(go_p, wout[...]).astype(BF16).astype(F32)
    low_lane = iota((128, 128), 1) < HEAD_DIM
    for i in range(3):
        qc = q_f[:, 128 * i : 128 * i + 128]
        gc = ga[:, 128 * i : 128 * i + 128]
        bdq[i, 0:128] = jnp.where(low_lane, qc, 0.0).astype(BF16)
        bdq[i, 128:256] = jnp.where(low_lane, 0.0, qc).astype(BF16)
        bdo[i, 0:128] = jnp.where(low_lane, gc, 0.0).astype(BF16)
        bdo[i, 128:256] = jnp.where(low_lane, 0.0, gc).astype(BF16)
    tot[...] = jnp.zeros_like(tot)
    dlt[...] = jnp.zeros_like(dlt)
    dq[...] = jnp.zeros_like(dq)

    lane2 = iota((1, 256), 1)
    scales = [
        jnp.where(lane2 < 128, logit[2 * i], logit[2 * i + 1]) * (1.0 / math.sqrt(HEAD_DIM))
        for i in range(3)
    ]
    edge = jnp.where(
        (iota((128, 256), 0) >= CELLS) == ((iota((128, 256), 1) & 127) >= CELLS), 1.0, 0.0
    )

    def pass1(p, g):
        sided = jnp.where((g == 1) | (g == 2) | (g == 4), 1.0, 0.0)
        bound = (1.0 - sided * (1.0 - edge)) * 64.0 - 32.0
        mask = None
        for i in range(3):
            keys = kv[p, pl.ds(2 * g, 2), :, 128 * i : 128 * i + 128].reshape(128, 128)
            vals = kv[p, pl.ds(2 * g, 2), :, WIDTH + 128 * i : WIDTH + 128 * i + 128].reshape(128, 128)
            if mask is None:
                mask = keys[:, 0:1].astype(F32) < bound
            s = nt(keys, bdq[i])
            e = jnp.where(mask, jnp.exp(s * scales[i]), 0.0)
            d = nt(vals, bdo[i])
            lanes = slice(256 * i, 256 * i + 256)
            ee[p, g, :, lanes] = e
            dd[p, g, :, lanes] = d
            tot[:, lanes] += jnp.sum(e.reshape(16, 8, 256), 0)
            dlt[:, lanes] += jnp.sum((e * d).reshape(16, 8, 256), 0)

    def here(g):
        return (g < 4) | x_from

    def wait_fwd(slot, c):
        j = (slot - 2) * CHUNKS + c
        dst = piece(kv, (1, slot), c)
        remote(dst, dst, fs.at[j], fr.at[j], ydev(1)).wait_recv()

    def wait_pair(first, p, g, c):
        j = first * CHUNKS + c
        dst = pair(kv, (p,), 2 * g, c)
        remote(dst, dst, fs.at[j], fr.at[j], ydev(1)).wait_recv()

    def gather_step(g, carry):
        @pl.when((g < 6) & here(g))
        def _():
            for c in range(CHUNKS):
                @pl.when((g >= 1) & (g < 5))
                def _(c=c):
                    wait_fwd(2 * g, c)
                    wait_fwd(2 * g + 1, c)

                @pl.when(g == 5)
                def _(c=c):
                    wait_pair(8, 1, 5, c)

                @pl.when(g == 1)
                def _(c=c):
                    fwd(2, 6, c, ydev(-1))
                    fwd(3, 7, c, ydev(1))

                    @pl.when(x_to & (lon > 0))
                    def _():
                        fwd(2, 8, c, xdev(far_fwd))

                    @pl.when(x_to & (lon < nl - 1))
                    def _():
                        fwd(3, 9, c, xdev(far_fwd))

                @pl.when((g == 2) & x_to)
                def _(c=c):
                    @pl.when(lon == 0)
                    def _():
                        fwd(4, 8, c, xdev(far_fwd))

                    @pl.when(lon == nl - 1)
                    def _():
                        fwd(5, 9, c, xdev(far_fwd))

                @pl.when((g == 3) & x_to)
                def _(c=c):
                    fwd_mid(c, xdev(far_fwd))

                @pl.when(g >= 1)
                def _(c=c):
                    fwd_z(g, c)

            pass1(1, g)

        @pl.when((g >= 2) & here(g - 2))
        def _():
            h = g - 2

            @pl.when(has_lo)
            def _():
                for c in range(CHUNKS):
                    wait_pair(9 + h, 0, h, c)
                pass1(0, h)

            @pl.when(has_hi)
            def _():
                for c in range(CHUNKS):
                    wait_pair(15 + h, 2, h, c)
                pass1(2, h)

        return carry

    lax.fori_loop(0, 8, gather_step, 0)

    inv_rows, dlt_rows = [], []
    for i in range(3):
        lanes = slice(256 * i, 256 * i + 256)
        inv = 1.0 / jnp.sum(tot[:, lanes], 0, keepdims=True)
        inv_rows.append(inv)
        dlt_rows.append(jnp.sum(dlt[:, lanes], 0, keepdims=True) * inv)

    def pass2(p, g):
        for i in range(3):
            lanes = slice(256 * i, 256 * i + 256)
            keys = kv[p, pl.ds(2 * g, 2), :, 128 * i : 128 * i + 128].reshape(128, 128)
            pr = ee[p, g, :, lanes] * inv_rows[i]
            ds = (pr * (dd[p, g, :, lanes] - dlt_rows[i]) * scales[i]).astype(BF16)
            dk = nn(ds, bdq[i]).reshape(2, CELLS, 128)
            dv = nn(pr.astype(BF16), bdo[i]).reshape(2, CELLS, 128)
            dq[i] += tn(ds, keys)
            klanes = slice(128 * i, 128 * i + 128)
            vlanes = slice(WIDTH + 128 * i, WIDTH + 128 * i + 128)
            if p == 1:
                acc[pl.ds(2 * g, 2), :, klanes] = dk
                acc[pl.ds(2 * g, 2), :, vlanes] = dv
            else:
                gs[p // 2, pl.ds(2 * g, 2), :, klanes] = dk.astype(BF16)
                gs[p // 2, pl.ds(2 * g, 2), :, vlanes] = dv.astype(BF16)

    def back_lo(g, c):
        j = (9 + g) * CHUNKS + c
        remote(
            pair(gs, (0,), 2 * g, c), pair(rz, (0,), 2 * g, c), bs.at[j], br.at[j], tdev(-1)
        ).start()

    def back_hi(g, c):
        j = (15 + g) * CHUNKS + c
        remote(
            pair(gs, (1,), 2 * g, c), pair(rz, (1,), 2 * g, c), bs.at[j], br.at[j], tdev(1)
        ).start()

    def wait_back(j, dst):
        remote(dst, dst, bs.at[j], br.at[j], ydev(1)).wait_recv()

    def rows_of(c):
        return pl.ds(ROWS * c, ROWS)

    def take_z(g, c):
        slots = pl.ds(2 * g, 2)

        @pl.when(has_hi)
        def _():
            wait_back((9 + g) * CHUNKS + c, pair(rz, (0,), 2 * g, c))
            acc[slots, rows_of(c)] += rz[0, slots, rows_of(c)].astype(F32)

        @pl.when(has_lo)
        def _():
            wait_back((15 + g) * CHUNKS + c, pair(rz, (1,), 2 * g, c))
            acc[slots, rows_of(c)] += rz[1, slots, rows_of(c)].astype(F32)

    def back(slot, base, sends, lands, c, dev):
        j = (slot - 2) * CHUNKS + c
        sends[slot - base, rows_of(c)] = acc[slot, rows_of(c)].astype(BF16)
        remote(
            piece(sends, (slot - base,), c), piece(lands, (slot - base,), c), bs.at[j], br.at[j], dev
        ).start()

    def take(slot, base, lands, c, into):
        wait_back((slot - 2) * CHUNKS + c, piece(lands, (slot - base,), c))
        acc[into, rows_of(c)] += lands[slot - base, rows_of(c)].astype(F32)

    def back_x(slot, c):
        back(slot, 8, xs, rx, c, xdev(-far_fwd))

    def take_x(slot, c, into):
        take(slot, 8, rx, c, into)

    def back_y(slot, c, dev):
        back(slot, 2, ys, ry, c, dev)

    def take_y(slot, c, into):
        take(slot, 2, ry, c, into)

    def back_mid(c):
        j = 8 * CHUNKS + c
        xs[2:4, rows_of(c)] = acc[10:12, rows_of(c)].astype(BF16)
        remote(
            pair(xs, (), 2, c), pair(rx, (), 2, c), bs.at[j], br.at[j], xdev(-far_fwd)
        ).start()

    def take_mid(c):
        wait_back(8 * CHUNKS + c, pair(rx, (), 2, c))
        acc[6:8, rows_of(c)] += rx[2:4, rows_of(c)].astype(F32)

    def far_back(c):
        take_z(5, c)
        back_mid(c)
        take_z(4, c)
        back_x(8, c)
        back_x(9, c)

    def back_step(k, carry):
        g = 5 - k + jnp.where(k == 4, 1, 0) - jnp.where(k == 3, 1, 0)

        @pl.when(here(g))
        def _():
            for p, there, send in ((0, has_lo, back_lo), (2, has_hi, back_hi)):
                @pl.when(there)
                def _(p=p, send=send):
                    pass2(p, g)
                    send(g, 0)
                    for c in range(1, CHUNKS):
                        pl.when(k == 1)(functools.partial(send, 5, c))
                        pl.when(k > 0)(functools.partial(send, g, c))

            pass2(1, g)

        @pl.when((k == 2) & x_from)
        def _():
            far_back(0)

        return carry

    lax.fori_loop(0, 6, back_step, 0)

    def drain(sems, first, count, whole):
        def one(j, carry):
            remote(whole, whole, sems.at[j], sems.at[j], ydev(1)).wait_send()
            return carry

        lax.fori_loop(first * CHUNKS, (first + count) * CHUNKS, one, 0)

    one_piece, two_pieces = piece(ys, (0,), 0), pair(gs, (0,), 0, 0)
    x_left, x_right = x_to & (lon > 0), x_to & (lon < nl - 1)
    x_left_end, x_right_end = x_to & (lon == 0), x_to & (lon == nl - 1)

    @pl.when(x_from)
    def _():
        for c in range(1, CHUNKS):
            far_back(c)

    for c in range(CHUNKS):
        take_z(3, c)
        pl.when(x_to)(functools.partial(take_mid, c))
        back_y(6, c, ydev(1))
        back_y(7, c, ydev(-1))

    def send_a5(c):
        take_z(1, c)
        pl.when(x_left)(functools.partial(take_x, 8, c, 2))
        pl.when(x_right)(functools.partial(take_x, 9, c, 3))
        take_y(6, c, 2)
        take_y(7, c, 3)
        back_y(2, c, ydev(nl - 1))
        back_y(3, c, ydev(1 - nl))

    def send_a1(c):
        take_z(2, c)
        pl.when(x_left_end)(functools.partial(take_x, 8, c, 4))
        pl.when(x_right_end)(functools.partial(take_x, 9, c, 5))
        back_y(4, c, ydev(-1))
        back_y(5, c, ydev(1))

    send_a5(0)
    for c in range(CHUNKS):
        send_a1(c)
    for c in range(1, CHUNKS):
        send_a5(c)
    for c in range(CHUNKS):
        take_z(0, c)
    drain(fs, 0, 6, one_piece)

    @pl.when(x_to)
    def _():
        drain(fs, 6, 2, one_piece)
        drain(fs, 8, 1, two_pieces)

    @pl.when(x_from)
    def _():
        drain(bs, 6, 2, one_piece)
        drain(bs, 8, 1, two_pieces)

    for sems, first, there in (
        (fs, 9, has_hi), (fs, 15, has_lo), (bs, 9, has_lo), (bs, 15, has_hi)
    ):
        pl.when(there)(functools.partial(drain, sems, first, 4, two_pieces))
        pl.when(there & x_from)(functools.partial(drain, sems, first + 4, 2, two_pieces))

    def rows_back(raw, inverse, grad):
        return inverse * grad - inverse * inverse * inverse * raw * nn_split(raw * grad, mean_mat)

    dq_full = jnp.concatenate(
        [jnp.where(low_lane, dq[i, 0:128], dq[i, 128:256]) for i in range(3)], axis=1
    )
    gn_q[...] = nt(rows_back(raw_s[0], raw_s[2], dq_full).astype(BF16), wqkv[0])

    for c in range(CHUNKS):
        take_y(4, c, 1)
        take_y(5, c, 0)
    for c in range(CHUNKS):
        take_y(2, c, 1)
        take_y(3, c, 0)
    drain(bs, 0, 6, one_piece)

    pair = acc[0:2].reshape(128, 2 * WIDTH)
    gk = rows_back(raw_s[1], raw_s[3], pair[:, :WIDTH]).astype(BF16)
    gv = pair[:, WIDTH:].astype(BF16)
    gn = gn_q[...] + nt(gk, wqkv[1]) + nt(gv, wqkv[2])
    g = gain[...][None, :] * gn
    xv = xp_s[...]
    r = rows_s[:, 0:1]
    res = r * g - r * r * r * xv * jnp.mean(xv * g, -1, keepdims=True)
    perm_back = (iota(shape2, 0) == original_row(iota(shape2, 1))).astype(F32).astype(BF16)
    out[...] = nn(perm_back, res.astype(BF16)).reshape(4, 4, 8, 768).astype(BF16)


def solution(mesh):
    nt_size, nlat, nl = mesh.shape["tm"], mesh.shape["lat"], mesh.shape["lon"]

    def per_device(tokens, key_count, norm_gain, qkv_weight, out_weight, logit_scale, grad_out):
        vmem = pl.BlockSpec(memory_space=pltpu.VMEM)
        smem = pl.BlockSpec(memory_space=pltpu.SMEM)
        hbm = pl.BlockSpec(memory_space=pl.ANY)
        block = (CELLS, 2 * WIDTH)
        return pl.pallas_call(
            functools.partial(kernel, nt_size, nlat // 2, nl),
            out_shape=jax.ShapeDtypeStruct(tokens.shape, BF16),
            in_specs=[smem, smem, vmem, hbm, hbm, hbm, hbm],
            out_specs=vmem,
            scratch_shapes=[
                pltpu.VMEM((3, 12) + block, BF16),
                pltpu.VMEM((3, 6, 128, 768), F32),
                pltpu.VMEM((3, 6, 128, 768), F32),
                pltpu.VMEM((2, 12) + block, BF16),
                pltpu.VMEM((12,) + block, F32),
                pltpu.VMEM((2, 12) + block, BF16),
                pltpu.VMEM((4,) + block, BF16),
                pltpu.VMEM((4,) + block, BF16),
                pltpu.VMEM((6,) + block, BF16),
                pltpu.VMEM((6,) + block, BF16),
                pltpu.VMEM((3, 256, 128), BF16),
                pltpu.VMEM((3, 256, 128), BF16),
                pltpu.VMEM((8, 768), F32),
                pltpu.VMEM((8, 768), F32),
                pltpu.VMEM((3, 256, 128), F32),
                pltpu.VMEM((128, 768), F32),
                pltpu.VMEM((128, 768), F32),
                pltpu.VMEM((4, 128, WIDTH), F32),
                pltpu.VMEM((128, 128), F32),
                pltpu.VMEM(tokens.shape, BF16),
                pltpu.VMEM(qkv_weight.shape, BF16),
                pltpu.VMEM(out_weight.shape, BF16),
                pltpu.VMEM(grad_out.shape, BF16),
                pltpu.SemaphoreType.DMA((21 * CHUNKS,)),
                pltpu.SemaphoreType.DMA((21 * CHUNKS,)),
                pltpu.SemaphoreType.DMA((21 * CHUNKS,)),
                pltpu.SemaphoreType.DMA((21 * CHUNKS,)),
                pltpu.SemaphoreType.DMA((6,)),
            ],
            compiler_params=pltpu.CompilerParams(
                collective_id=0, has_side_effects=True, vmem_limit_bytes=56 * 1024 * 1024
            ),
        )(
            key_count, logit_scale, norm_gain, tokens, qkv_weight, out_weight, grad_out,
        )

    split = P("tm", "lat", "lon", None)
    return jax.shard_map(
        per_device,
        mesh=mesh,
        in_specs=(split, P("tm", "lat", "lon"), P(), P(), P(), P(), split),
        out_specs=split,
        check_vma=False,
    )
```

```python
import functools
import math

import jax
import jax.numpy as jnp
from jax import lax
from jax.experimental import pallas as pl
from jax.experimental.pallas import tpu as pltpu
from jax.sharding import PartitionSpec as P

MESH = pl.DeviceIdType.MESH
F32 = jnp.float32
BF16 = jnp.bfloat16
HEADS = 6
HEAD_DIM = 64
WIDTH = HEADS * HEAD_DIM
CELLS = 64
EPS = 1e-6
DEAD = 64.0
CHUNKS = 2
ROWS = CELLS // CHUNKS


def nt(a, b):
    return lax.dot_general(a, b, (((1,), (1,)), ((), ())), preferred_element_type=F32)


def tn(a, b):
    return lax.dot_general(a, b, (((0,), (0,)), ((), ())), preferred_element_type=F32)


def nn(a, b):
    return lax.dot_general(a, b, (((1,), (0,)), ((), ())), preferred_element_type=F32)


def nn_split(a, b):
    high = a.astype(BF16)
    return nn(high, b) + nn((a - high.astype(F32)).astype(BF16), b)


def iota(shape, dim):
    return lax.broadcasted_iota(jnp.int32, shape, dim)


def original_row(p):
    return (
        (((p >> 4) & 3) << 5) + (((p >> 2) & 3) << 3) + (((p >> 6) & 1) << 2) + (p & 3)
    )


def head_mean():
    shape = (WIDTH, WIDTH)
    return jnp.where(
        (iota(shape, 0) >> 6) == (iota(shape, 1) >> 6), 1.0 / HEAD_DIM, 0.0
    ).astype(BF16)


def kernel(
    nt_size, nx, nl,
    count, logit, gain, tok_h, w_h, wout_h, gout_h, out,
    kv, ee, dd, gs, acc, rz, xs, rx, ys, ry, bdq, bdo, tot, dlt, dq,
    xp_s, gn_q, raw_s, rows_s, tok, wqkv, wout, gout,
    fs, fr, bs, br, ins,
):
    tm = lax.axis_index("tm")
    lat = lax.axis_index("lat")
    lon = lax.axis_index("lon")
    x, yh = lat // 2, lat % 2
    y = yh * nl + lon
    ny = 2 * nl

    def ydev(k):
        yy = (y + k + ny) % ny
        return (tm, x * 2 + yy // nl, yy % nl)

    def xdev(k):
        return (tm, (x + k) * 2 + yh, lon)

    def tdev(k):
        return (tm + k, lat, lon)

    far_fwd = 1 - 2 * yh
    has_lo, has_hi = tm > 0, tm < nt_size - 1
    x_lo, x_hi = x > 0, x < nx - 1
    x_to = ((yh == 0) & x_hi) | ((yh == 1) & x_lo)
    x_from = ((yh == 0) & x_lo) | ((yh == 1) & x_hi)

    barrier = pltpu.get_barrier_semaphore()

    def greet(dev):
        pl.semaphore_signal(barrier, inc=1, device_id=dev, device_id_type=MESH)

    for k in (1, -1, nl - 1, 1 - nl):
        greet(ydev(k))
    for there, dev in ((x_lo, xdev(-1)), (x_hi, xdev(1)), (has_lo, tdev(-1)), (has_hi, tdev(1))):
        pl.when(there)(functools.partial(greet, dev))
    greeted = (
        4 + jnp.minimum(x, 1) + jnp.minimum(nx - 1 - x, 1)
        + jnp.minimum(tm, 1) + jnp.minimum(nt_size - 1 - tm, 1)
    )

    loads = [
        pltpu.make_async_copy(src, dst, ins.at[n])
        for n, (src, dst) in enumerate((
            (tok_h, tok), (w_h.at[1], wqkv.at[1]), (w_h.at[2], wqkv.at[2]),
            (w_h.at[0], wqkv.at[0]), (gout_h, gout), (wout_h, wout),
        ))
    ]
    for load in loads[:3]:
        load.start()

    shape2 = (128, 128)
    perm = (iota(shape2, 1) == original_row(iota(shape2, 0))).astype(F32).astype(BF16)
    mean_mat = head_mean()
    loads[0].wait()
    xp = nn(perm, tok[...].astype(F32).reshape(128, 768).astype(BF16))
    row_inv = lax.rsqrt(jnp.mean(xp * xp, -1, keepdims=True) + EPS)
    normed = (xp * row_inv * gain[...][None, :]).astype(BF16)
    loads[1].wait()
    for load in loads[3:]:
        load.start()
    k_raw = nn(normed, wqkv[1])
    k_inv = lax.rsqrt(nn_split(k_raw * k_raw, mean_mat) + EPS)
    loads[2].wait()
    v_bf = nn(normed, wqkv[2]).astype(BF16)
    row1 = iota((128, 1), 0)
    limit = jnp.where(row1 < CELLS, count[0, 0, 0], count[0, 0, 1])
    live = (row1 & (CELLS - 1)) < limit
    k_bf = jnp.where(live, k_raw * k_inv, DEAD).astype(BF16)
    kv[1, 0, :, 0:WIDTH] = k_bf[:CELLS]
    kv[1, 1, :, 0:WIDTH] = k_bf[CELLS:]
    kv[1, 0, :, WIDTH:] = v_bf[:CELLS]
    kv[1, 1, :, WIDTH:] = v_bf[CELLS:]

    def piece(ref, index, c):
        return ref.at[index + (pl.ds(ROWS * c, ROWS),)]

    def remote(src, dst, send, recv, dev):
        return pltpu.make_async_remote_copy(
            src_ref=src, dst_ref=dst, send_sem=send, recv_sem=recv,
            device_id=dev, device_id_type=MESH,
        )

    def fwd(src_slot, dst_slot, c, dev):
        j = (dst_slot - 2) * CHUNKS + c
        remote(
            piece(kv, (1, src_slot), c), piece(kv, (1, dst_slot), c), fs.at[j], fr.at[j], dev
        ).start()

    def pair(ref, index, first, c):
        return ref.at[index + (pl.ds(first, 2), pl.ds(ROWS * c, ROWS))]

    def fwd_mid(c, dev):
        j = 8 * CHUNKS + c
        remote(
            pair(kv, (1,), 6, c), pair(kv, (1,), 10, c), fs.at[j], fr.at[j], dev
        ).start()

    def fwd_z(g, c):
        lo, hi = (9 + g) * CHUNKS + c, (15 + g) * CHUNKS + c
        src = pair(kv, (1,), 2 * g, c)

        @pl.when(has_hi)
        def _():
            remote(src, pair(kv, (0,), 2 * g, c), fs.at[lo], fr.at[lo], tdev(1)).start()

        @pl.when(has_lo)
        def _():
            remote(src, pair(kv, (2,), 2 * g, c), fs.at[hi], fr.at[hi], tdev(-1)).start()

    pl.semaphore_wait(barrier, greeted)
    for c in range(CHUNKS):
        fwd(1, 2, c, ydev(1 - nl))
        fwd(0, 3, c, ydev(nl - 1))
    for c in range(CHUNKS):
        fwd(1, 4, c, ydev(1))
        fwd(0, 5, c, ydev(-1))
    for c in range(CHUNKS):
        fwd_z(0, c)

    xp_s[...] = xp
    rows_s[...] = jnp.broadcast_to(row_inv, (128, 128))
    loads[3].wait()
    q_raw = nn(normed, wqkv[0])
    q_inv = lax.rsqrt(nn_split(q_raw * q_raw, mean_mat) + EPS)
    raw_s[0] = q_raw
    raw_s[1] = k_raw
    raw_s[2] = q_inv
    raw_s[3] = k_inv
    q_f = q_raw * q_inv
    loads[4].wait()
    go_p = nn(perm, gout[...].astype(F32).reshape(128, 768).astype(BF16)).astype(BF16)
    loads[5].wait()
    ga = nt(go_p, wout[...]).astype(BF16).astype(F32)
    low_lane = iota((128, 128), 1) < HEAD_DIM
    for i in range(3):
        qc = q_f[:, 128 * i : 128 * i + 128]
        gc = ga[:, 128 * i : 128 * i + 128]
        bdq[i, 0:128] = jnp.where(low_lane, qc, 0.0).astype(BF16)
        bdq[i, 128:256] = jnp.where(low_lane, 0.0, qc).astype(BF16)
        bdo[i, 0:128] = jnp.where(low_lane, gc, 0.0).astype(BF16)
        bdo[i, 128:256] = jnp.where(low_lane, 0.0, gc).astype(BF16)
    tot[...] = jnp.zeros_like(tot)
    dlt[...] = jnp.zeros_like(dlt)
    dq[...] = jnp.zeros_like(dq)

    lane2 = iota((1, 256), 1)
    scales = [
        jnp.where(lane2 < 128, logit[2 * i], logit[2 * i + 1]) * (1.0 / math.sqrt(HEAD_DIM))
        for i in range(3)
    ]
    edge = jnp.where(
        (iota((128, 256), 0) >= CELLS) == ((iota((128, 256), 1) & 127) >= CELLS), 1.0, 0.0
    )

    def pass1(p, g):
        sided = jnp.where((g == 1) | (g == 2) | (g == 4), 1.0, 0.0)
        bound = (1.0 - sided * (1.0 - edge)) * 64.0 - 32.0
        mask = None
        for i in range(3):
            keys = kv[p, pl.ds(2 * g, 2), :, 128 * i : 128 * i + 128].reshape(128, 128)
            vals = kv[p, pl.ds(2 * g, 2), :, WIDTH + 128 * i : WIDTH + 128 * i + 128].reshape(128, 128)
            if mask is None:
                mask = keys[:, 0:1].astype(F32) < bound
            s = nt(keys, bdq[i])
            e = jnp.where(mask, jnp.exp(s * scales[i]), 0.0)
            d = nt(vals, bdo[i])
            lanes = slice(256 * i, 256 * i + 256)
            ee[p, g, :, lanes] = e
            dd[p, g, :, lanes] = d
            tot[:, lanes] += jnp.sum(e.reshape(16, 8, 256), 0)
            dlt[:, lanes] += jnp.sum((e * d).reshape(16, 8, 256), 0)

    def here(g):
        return (g < 4) | x_from

    def wait_fwd(slot, c):
        j = (slot - 2) * CHUNKS + c
        dst = piece(kv, (1, slot), c)
        remote(dst, dst, fs.at[j], fr.at[j], ydev(1)).wait_recv()

    def wait_pair(first, p, g, c):
        j = first * CHUNKS + c
        dst = pair(kv, (p,), 2 * g, c)
        remote(dst, dst, fs.at[j], fr.at[j], ydev(1)).wait_recv()

    def gather_step(g, carry):
        @pl.when((g < 6) & here(g))
        def _():
            for c in range(CHUNKS):
                @pl.when((g >= 1) & (g < 5))
                def _(c=c):
                    wait_fwd(2 * g, c)
                    wait_fwd(2 * g + 1, c)

                @pl.when(g == 5)
                def _(c=c):
                    wait_pair(8, 1, 5, c)

                @pl.when(g == 1)
                def _(c=c):
                    fwd(2, 6, c, ydev(-1))
                    fwd(3, 7, c, ydev(1))

                    @pl.when(x_to & (lon > 0))
                    def _():
                        fwd(2, 8, c, xdev(far_fwd))

                    @pl.when(x_to & (lon < nl - 1))
                    def _():
                        fwd(3, 9, c, xdev(far_fwd))

                @pl.when((g == 2) & x_to)
                def _(c=c):
                    @pl.when(lon == 0)
                    def _():
                        fwd(4, 8, c, xdev(far_fwd))

                    @pl.when(lon == nl - 1)
                    def _():
                        fwd(5, 9, c, xdev(far_fwd))

                @pl.when((g == 3) & x_to)
                def _(c=c):
                    fwd_mid(c, xdev(far_fwd))

                @pl.when(g >= 1)
                def _(c=c):
                    fwd_z(g, c)

            pass1(1, g)

        @pl.when((g >= 2) & here(g - 2))
        def _():
            h = g - 2

            @pl.when(has_lo)
            def _():
                for c in range(CHUNKS):
                    wait_pair(9 + h, 0, h, c)
                pass1(0, h)

            @pl.when(has_hi)
            def _():
                for c in range(CHUNKS):
                    wait_pair(15 + h, 2, h, c)
                pass1(2, h)

        return carry

    lax.fori_loop(0, 8, gather_step, 0)

    inv_rows, dlt_rows = [], []
    for i in range(3):
        lanes = slice(256 * i, 256 * i + 256)
        inv = 1.0 / jnp.sum(tot[:, lanes], 0, keepdims=True)
        inv_rows.append(inv)
        dlt_rows.append(jnp.sum(dlt[:, lanes], 0, keepdims=True) * inv)

    def pass2(p, g):
        for i in range(3):
            lanes = slice(256 * i, 256 * i + 256)
            keys = kv[p, pl.ds(2 * g, 2), :, 128 * i : 128 * i + 128].reshape(128, 128)
            pr = ee[p, g, :, lanes] * inv_rows[i]
            ds = (pr * (dd[p, g, :, lanes] - dlt_rows[i]) * scales[i]).astype(BF16)
            dk = nn(ds, bdq[i]).reshape(2, CELLS, 128)
            dv = nn(pr.astype(BF16), bdo[i]).reshape(2, CELLS, 128)
            dq[i] += tn(ds, keys)
            klanes = slice(128 * i, 128 * i + 128)
            vlanes = slice(WIDTH + 128 * i, WIDTH + 128 * i + 128)
            if p == 1:
                acc[pl.ds(2 * g, 2), :, klanes] = dk
                acc[pl.ds(2 * g, 2), :, vlanes] = dv
            else:
                gs[p // 2, pl.ds(2 * g, 2), :, klanes] = dk.astype(BF16)
                gs[p // 2, pl.ds(2 * g, 2), :, vlanes] = dv.astype(BF16)

    def back_lo(g, c):
        j = (9 + g) * CHUNKS + c
        remote(
            pair(gs, (0,), 2 * g, c), pair(rz, (0,), 2 * g, c), bs.at[j], br.at[j], tdev(-1)
        ).start()

    def back_hi(g, c):
        j = (15 + g) * CHUNKS + c
        remote(
            pair(gs, (1,), 2 * g, c), pair(rz, (1,), 2 * g, c), bs.at[j], br.at[j], tdev(1)
        ).start()

    def wait_back(j, dst):
        remote(dst, dst, bs.at[j], br.at[j], ydev(1)).wait_recv()

    def rows_of(c):
        return pl.ds(ROWS * c, ROWS)

    def take_z(g, c):
        slots = pl.ds(2 * g, 2)

        @pl.when(has_hi)
        def _():
            wait_back((9 + g) * CHUNKS + c, pair(rz, (0,), 2 * g, c))
            acc[slots, rows_of(c)] += rz[0, slots, rows_of(c)].astype(F32)

        @pl.when(has_lo)
        def _():
            wait_back((15 + g) * CHUNKS + c, pair(rz, (1,), 2 * g, c))
            acc[slots, rows_of(c)] += rz[1, slots, rows_of(c)].astype(F32)

    def back(slot, base, sends, lands, c, dev):
        j = (slot - 2) * CHUNKS + c
        sends[slot - base, rows_of(c)] = acc[slot, rows_of(c)].astype(BF16)
        remote(
            piece(sends, (slot - base,), c), piece(lands, (slot - base,), c), bs.at[j], br.at[j], dev
        ).start()

    def take(slot, base, lands, c, into):
        wait_back((slot - 2) * CHUNKS + c, piece(lands, (slot - base,), c))
        acc[into, rows_of(c)] += lands[slot - base, rows_of(c)].astype(F32)

    def back_x(slot, c):
        back(slot, 8, xs, rx, c, xdev(-far_fwd))

    def take_x(slot, c, into):
        take(slot, 8, rx, c, into)

    def back_y(slot, c, dev):
        back(slot, 2, ys, ry, c, dev)

    def take_y(slot, c, into):
        take(slot, 2, ry, c, into)

    def back_mid(c):
        j = 8 * CHUNKS + c
        xs[2:4, rows_of(c)] = acc[10:12, rows_of(c)].astype(BF16)
        remote(
            pair(xs, (), 2, c), pair(rx, (), 2, c), bs.at[j], br.at[j], xdev(-far_fwd)
        ).start()

    def take_mid(c):
        wait_back(8 * CHUNKS + c, pair(rx, (), 2, c))
        acc[6:8, rows_of(c)] += rx[2:4, rows_of(c)].astype(F32)

    def far_back(c):
        take_z(5, c)
        back_mid(c)
        take_z(4, c)
        back_x(8, c)
        back_x(9, c)

    def back_step(k, carry):
        g = 5 - k + jnp.where(k == 4, 1, 0) - jnp.where(k == 3, 1, 0)

        @pl.when(here(g))
        def _():
            for p, there, send in ((0, has_lo, back_lo), (2, has_hi, back_hi)):
                @pl.when(there)
                def _(p=p, send=send):
                    pass2(p, g)
                    send(g, 0)
                    for c in range(1, CHUNKS):
                        pl.when(k == 1)(functools.partial(send, 5, c))
                        pl.when(k > 0)(functools.partial(send, g, c))

            pass2(1, g)

        @pl.when((k == 2) & x_from)
        def _():
            far_back(0)

        return carry

    lax.fori_loop(0, 6, back_step, 0)

    def drain(sems, first, count, whole):
        def one(j, carry):
            remote(whole, whole, sems.at[j], sems.at[j], ydev(1)).wait_send()
            return carry

        lax.fori_loop(first * CHUNKS, (first + count) * CHUNKS, one, 0)

    one_piece, two_pieces = piece(ys, (0,), 0), pair(gs, (0,), 0, 0)
    x_left, x_right = x_to & (lon > 0), x_to & (lon < nl - 1)
    x_left_end, x_right_end = x_to & (lon == 0), x_to & (lon == nl - 1)

    @pl.when(x_from)
    def _():
        for c in range(1, CHUNKS):
            far_back(c)

    for c in range(CHUNKS):
        take_z(3, c)
        pl.when(x_to)(functools.partial(take_mid, c))
        back_y(6, c, ydev(1))
        back_y(7, c, ydev(-1))

    def send_a5(c):
        take_z(1, c)
        pl.when(x_left)(functools.partial(take_x, 8, c, 2))
        pl.when(x_right)(functools.partial(take_x, 9, c, 3))
        take_y(6, c, 2)
        take_y(7, c, 3)
        back_y(2, c, ydev(nl - 1))
        back_y(3, c, ydev(1 - nl))

    def send_a1(c):
        take_z(2, c)
        pl.when(x_left_end)(functools.partial(take_x, 8, c, 4))
        pl.when(x_right_end)(functools.partial(take_x, 9, c, 5))
        back_y(4, c, ydev(-1))
        back_y(5, c, ydev(1))

    send_a5(0)
    for c in range(CHUNKS):
        send_a1(c)
    for c in range(1, CHUNKS):
        send_a5(c)
    for c in range(CHUNKS):
        take_z(0, c)
    drain(fs, 0, 6, one_piece)

    @pl.when(x_to)
    def _():
        drain(fs, 6, 2, one_piece)
        drain(fs, 8, 1, two_pieces)

    @pl.when(x_from)
    def _():
        drain(bs, 6, 2, one_piece)
        drain(bs, 8, 1, two_pieces)

    for sems, first, there in (
        (fs, 9, has_hi), (fs, 15, has_lo), (bs, 9, has_lo), (bs, 15, has_hi)
    ):
        pl.when(there)(functools.partial(drain, sems, first, 4, two_pieces))
        pl.when(there & x_from)(functools.partial(drain, sems, first + 4, 2, two_pieces))

    def rows_back(raw, inverse, grad):
        return inverse * grad - inverse * inverse * inverse * raw * nn_split(raw * grad, mean_mat)

    dq_full = jnp.concatenate(
        [jnp.where(low_lane, dq[i, 0:128], dq[i, 128:256]) for i in range(3)], axis=1
    )
    gn_q[...] = nt(rows_back(raw_s[0], raw_s[2], dq_full).astype(BF16), wqkv[0])

    for c in range(CHUNKS):
        take_y(4, c, 1)
        take_y(5, c, 0)
    def rows_at(ref, index, c):
        return jnp.concatenate(
            [ref[index + (pl.ds(CELLS * b + ROWS * c, ROWS),)] for b in range(2)], axis=0
        )

    for c in range(CHUNKS):
        take_y(2, c, 1)
        take_y(3, c, 0)
        both = acc[0:2, rows_of(c)].reshape(2 * ROWS, 2 * WIDTH)
        gk = rows_back(
            rows_at(raw_s, (1,), c), rows_at(raw_s, (3,), c), both[:, :WIDTH]
        ).astype(BF16)
        gv = both[:, WIDTH:].astype(BF16)
        g = gain[...][None, :] * (rows_at(gn_q, (), c) + nt(gk, wqkv[1]) + nt(gv, wqkv[2]))
        xv = rows_at(xp_s, (), c)
        r = rows_at(rows_s, (), c)[:, 0:1]
        res = r * g - r * r * r * xv * jnp.mean(xv * g, -1, keepdims=True)
        for b in range(2):
            xp_s[pl.ds(CELLS * b + ROWS * c, ROWS)] = res[ROWS * b : ROWS * b + ROWS]
    perm_back = (iota(shape2, 0) == original_row(iota(shape2, 1))).astype(F32).astype(BF16)
    out[...] = nn(perm_back, xp_s[...].astype(BF16)).reshape(4, 4, 8, 768).astype(BF16)
    drain(bs, 0, 6, one_piece)


def solution(mesh):
    nt_size, nlat, nl = mesh.shape["tm"], mesh.shape["lat"], mesh.shape["lon"]

    def per_device(tokens, key_count, norm_gain, qkv_weight, out_weight, logit_scale, grad_out):
        vmem = pl.BlockSpec(memory_space=pltpu.VMEM)
        smem = pl.BlockSpec(memory_space=pltpu.SMEM)
        hbm = pl.BlockSpec(memory_space=pl.ANY)
        block = (CELLS, 2 * WIDTH)
        return pl.pallas_call(
            functools.partial(kernel, nt_size, nlat // 2, nl),
            out_shape=jax.ShapeDtypeStruct(tokens.shape, BF16),
            in_specs=[smem, smem, vmem, hbm, hbm, hbm, hbm],
            out_specs=vmem,
            scratch_shapes=[
                pltpu.VMEM((3, 12) + block, BF16),
                pltpu.VMEM((3, 6, 128, 768), F32),
                pltpu.VMEM((3, 6, 128, 768), F32),
                pltpu.VMEM((2, 12) + block, BF16),
                pltpu.VMEM((12,) + block, F32),
                pltpu.VMEM((2, 12) + block, BF16),
                pltpu.VMEM((4,) + block, BF16),
                pltpu.VMEM((4,) + block, BF16),
                pltpu.VMEM((6,) + block, BF16),
                pltpu.VMEM((6,) + block, BF16),
                pltpu.VMEM((3, 256, 128), BF16),
                pltpu.VMEM((3, 256, 128), BF16),
                pltpu.VMEM((8, 768), F32),
                pltpu.VMEM((8, 768), F32),
                pltpu.VMEM((3, 256, 128), F32),
                pltpu.VMEM((128, 768), F32),
                pltpu.VMEM((128, 768), F32),
                pltpu.VMEM((4, 128, WIDTH), F32),
                pltpu.VMEM((128, 128), F32),
                pltpu.VMEM(tokens.shape, BF16),
                pltpu.VMEM(qkv_weight.shape, BF16),
                pltpu.VMEM(out_weight.shape, BF16),
                pltpu.VMEM(grad_out.shape, BF16),
                pltpu.SemaphoreType.DMA((21 * CHUNKS,)),
                pltpu.SemaphoreType.DMA((21 * CHUNKS,)),
                pltpu.SemaphoreType.DMA((21 * CHUNKS,)),
                pltpu.SemaphoreType.DMA((21 * CHUNKS,)),
                pltpu.SemaphoreType.DMA((6,)),
            ],
            compiler_params=pltpu.CompilerParams(
                collective_id=0, has_side_effects=True, vmem_limit_bytes=56 * 1024 * 1024
            ),
        )(
            key_count, logit_scale, norm_gain, tokens, qkv_weight, out_weight, grad_out,
        )

    split = P("tm", "lat", "lon", None)
    return jax.shard_map(
        per_device,
        mesh=mesh,
        in_specs=(split, P("tm", "lat", "lon"), P(), P(), P(), P(), split),
        out_specs=split,
        check_vma=False,
    )
```
